32 devices in a mesh: grp: 16 (over z, y, core), sub: 2 (over x).
Axes of the slice: x: 2, y: 2, z: 4, core: 2. Of those that a mesh axis runs over, the one named last changes fastest.
Arguments:
- state_zero: float32 [352, 16807], P(('grp', 'sub')), as said below
- state_one: float32 [224, 7776], P(('grp', 'sub')), as said below
- state_two: float32 [224, 7776], P(('grp', 'sub')), as said below
- state_three: float32 [128, 3125], P(('grp', 'sub')), as said below
- intra_zero: float32 [8, 7, 7], replicated, may hold values from -0.75 to 0.75
- intra_one: float32 [8, 6, 6], replicated, may hold values from -0.875 to 0.875
- intra_two: float32 [8, 6, 6], replicated, may hold values from -0.875 to 0.875
- intra_three: float32 [8, 5, 5], replicated, may hold values from -1 to 1
- intersections: float32 [3, 8, 7, 7], replicated, may hold values from -2 to 2
- positions: float32 [3, 8, 7, 7], replicated, may hold values from -2 to 2
- coupling_pair: int32 [24], replicated, may hold values from 0 to 2
- coupling_mode: int32 [24], replicated, may hold values from 0 to 7
- coupling_strength: float32 [24], replicated, may hold values from -3 to 3
Outputs:
- stepped_zero: float32 [352, 16807], P(('grp', 'sub'))
- stepped_one: float32 [224, 7776], P(('grp', 'sub'))
- stepped_two: float32 [224, 7776], P(('grp', 'sub'))
- stepped_three: float32 [128, 3125], P(('grp', 'sub'))
- density_zero: float32 [8, 7, 7], replicated
- density_one: float32 [8, 6, 6], replicated
- density_two: float32 [8, 6, 6], replicated
- density_three: float32 [8, 5, 5], replicated
The draws below stay inside these ranges and needn't reach their ends.
Inputs may be any that keep to these rules, and one draw needn't show every extreme that they name: `state_zero`: rows from 7**3 on are zero. `state_one`: rows from 6**3 on are zero. `state_two`: rows from 6**3 on are zero. `state_three`: rows from 5**3 on are zero.
All inputs are finite; a program needn't handle non-finite values.
Results may differ from the reference program's by a relative error of at most 0.0001.
Values sent between devices are 32-bit elements; how exact they have to be, the bound alone decides.
A program may use at most 256 MiB of HBM per device.

```python
import math
import jax
import jax.numpy as jnp
from jax import lax

N0 = 7
N1 = 6
N2 = 6
N3 = 5
F = 8
PAIRS = 3
TERMS = 24
PAD0 = 352
PAD1 = 224
PAD2 = 224
PAD3 = 128


def state_draw(key, mode_width, rows_total):
    real_rows = mode_width ** 3
    columns = mode_width ** 5
    value_key, column_key = jax.random.split(key)
    row_pos = jnp.arange(rows_total).astype(jnp.float32)
    values = jax.random.normal(value_key, (rows_total, columns), jnp.float32)
    row_scale = 10.0 ** (row_pos / real_rows)
    divisor = 20.0
    live_rows = (row_pos < real_rows).astype(jnp.float32)
    tail_pos = (jnp.arange(columns) % real_rows).astype(jnp.float32)
    jitter = jax.random.uniform(column_key, (columns,), jnp.float32)
    column_scale = 10.0 ** (0.7 * tail_pos / real_rows + 0.3 * jitter)
    return values * (row_scale * live_rows)[:, None] * column_scale[None, :] / divisor


def draw_state_zero(key, part):
    return state_draw(jax.random.fold_in(key, 101), N0, PAD0)


def draw_state_one(key, part):
    return state_draw(jax.random.fold_in(key, 202), N1, PAD1)


def draw_state_two(key, part):
    return state_draw(jax.random.fold_in(key, 303), N2, PAD2)


def draw_state_three(key, part):
    return state_draw(jax.random.fold_in(key, 404), N3, PAD3)


def place_ends(entries, stream_key, low, largest):
    index_at = [jax.random.randint(jax.random.fold_in(stream_key, axis), (), 0, length) for axis, length in enumerate(entries.shape)]
    main_axis = entries.shape.index(max(entries.shape))
    neighbour = index_at[:main_axis] + [(index_at[main_axis] + 1) % entries.shape[main_axis]] + index_at[main_axis + 1:]
    return entries.at[tuple(index_at)].set(low).at[tuple(neighbour)].set(largest)


def scatter_about(own_key, extent, spread, limit, kind=jnp.bfloat16):
    entries = jax.random.normal(own_key, extent, jnp.float32) * spread
    return jnp.minimum(jnp.maximum(entries, -limit), limit).astype(kind)


def setup_inputs(seed: int = 0) -> dict:
    keys = jax.random.split(jax.random.key(seed), 14)
    return {
        "state_zero": draw_state_zero(jax.random.fold_in(keys[13], 71), 0),
        "state_one": draw_state_one(jax.random.fold_in(keys[13], 71), 0),
        "state_two": draw_state_two(jax.random.fold_in(keys[13], 71), 0),
        "state_three": draw_state_three(jax.random.fold_in(keys[13], 71), 0),
        "intra_zero": scatter_about(keys[4], (F, N0, N0), (F * N0) ** -0.5, 0.75, jnp.float32),
        "intra_one": scatter_about(keys[5], (F, N1, N1), (F * N1) ** -0.5, 0.875, jnp.float32),
        "intra_two": scatter_about(keys[6], (F, N2, N2), (F * N2) ** -0.5, 0.875, jnp.float32),
        "intra_three": scatter_about(keys[7], (F, N3, N3), (F * N3) ** -0.5, 1.0, jnp.float32),
        "intersections": scatter_about(keys[8], (PAIRS, F, N0, N0), N0 ** -0.5, 2.0, jnp.float32),
        "positions": scatter_about(keys[9], (PAIRS, F, N0, N0), N0 ** -0.5, 2.0, jnp.float32),
        "coupling_pair": place_ends(jax.random.randint(keys[10], (TERMS,), 0, PAIRS), jax.random.fold_in(keys[10], 1), 0, PAIRS - 1).astype(jnp.int32),
        "coupling_mode": place_ends(jax.random.randint(keys[11], (TERMS,), 0, F), jax.random.fold_in(keys[11], 1), 0, F - 1).astype(jnp.int32),
        "coupling_strength": scatter_about(keys[12], (TERMS,), 0.5, 3.0, jnp.float32),
    }


highest = lax.Precision.HIGHEST
time_step = 0.25


def along_mode(tensor, matrix, axis_at):
    old_shape = tensor.shape
    before = math.prod(old_shape[:axis_at])
    behind = math.prod(old_shape[axis_at + 1:])
    shaped = tensor.reshape(before, old_shape[axis_at], behind)
    result = jnp.einsum("ab,xby->xay", matrix, shaped, precision=highest)
    return result.reshape(old_shape[:axis_at] + (matrix.shape[0],) + old_shape[axis_at + 1:])


def coupled(source, over_mats, pos_mats, weights):
    zero_part = source
    one_part = None
    modes_count = source.ndim
    for axis_at in range(modes_count):
        moved_part = weights[axis_at] * along_mode(zero_part, pos_mats[axis_at], axis_at)
        if one_part is not None:
            moved_part = along_mode(one_part, over_mats[axis_at], axis_at) + moved_part
        if axis_at + 1 < modes_count:
            zero_part = along_mode(zero_part, over_mats[axis_at], axis_at)
        one_part = moved_part
    return one_part


def intra(tensor, operator_set):
    summed = jnp.zeros_like(tensor)
    for axis_at in range(tensor.ndim):
        summed = summed + along_mode(tensor, operator_set[axis_at], axis_at)
    return summed


def density(tensor):
    mode_width = tensor.shape[0]
    per_mode = []
    for axis_at in range(tensor.ndim):
        before = mode_width ** axis_at
        behind = mode_width ** (tensor.ndim - 1 - axis_at)
        shaped = tensor.reshape(before, mode_width, behind)
        per_mode.append(jnp.einsum("xiy,xjy->ij", shaped, shaped, precision=highest))
    return jnp.stack(per_mode) / float(mode_width ** (tensor.ndim - 1))


def reference(state_zero, state_one, state_two, state_three, intra_zero, intra_one, intra_two, intra_three, intersections, positions, coupling_pair, coupling_mode, coupling_strength):
    packed = [state_zero, state_one, state_two, state_three]
    operators = [intra_zero, intra_one, intra_two, intra_three]
    padded_rows = [PAD0, PAD1, PAD2, PAD3]
    widths = [N0, N1, N2, N3]
    tensors = []
    for state_index in range(4):
        span_rows = widths[state_index] ** 3
        tensors.append(packed[state_index][:span_rows].reshape((widths[state_index],) * F))
    pair_pick = (coupling_pair[:, None] == jnp.arange(PAIRS, dtype=jnp.int32)[None, :]).astype(coupling_strength.dtype)
    mode_pick = (coupling_mode[:, None] == jnp.arange(F, dtype=jnp.int32)[None, :]).astype(coupling_strength.dtype)
    weight_table = jnp.einsum("t,tp,tk->pk", coupling_strength, pair_pick, mode_pick, precision=highest)
    actions = [intra(tensors[state_index], operators[state_index]) for state_index in range(4)]
    for pair_index in range(PAIRS):
        lower_state = pair_index
        upper_state = pair_index + 1
        over_mats = intersections[pair_index, :, :widths[lower_state], :widths[upper_state]]
        pos_mats = positions[pair_index, :, :widths[lower_state], :widths[upper_state]]
        actions[lower_state] = actions[lower_state] + coupled(tensors[upper_state], over_mats, pos_mats, weight_table[pair_index])
        actions[upper_state] = actions[upper_state] + coupled(tensors[lower_state], jnp.transpose(over_mats, (0, 2, 1)), jnp.transpose(pos_mats, (0, 2, 1)), weight_table[pair_index])
    outputs = []
    densities = []
    for state_index in range(4):
        mode_width = widths[state_index]
        stepped = (tensors[state_index] - time_step * actions[state_index]).reshape(mode_width ** 3, mode_width ** (F - 3))
        filler = jnp.zeros((padded_rows[state_index] - mode_width ** 3, mode_width ** (F - 3)), stepped.dtype)
        outputs.append(jnp.concatenate([stepped, filler], axis=0))
        densities.append(density(tensors[state_index]))
    return (outputs[0], outputs[1], outputs[2], outputs[3], densities[0], densities[1], densities[2], densities[3])
```

```python
import functools
import math

import jax
import jax.numpy as jnp
import numpy as np
from jax import lax
from jax.experimental import pallas as pl
from jax.experimental.pallas import tpu as pltpu
from jax.sharding import PartitionSpec as P

highest = lax.Precision.HIGHEST
high = lax.Precision.HIGH
time_step = 0.25
lanes = 128
vmem_limit = 60 * 1024 * 1024
params = pltpu.CompilerParams(vmem_limit_bytes=vmem_limit)
vmem = pl.BlockSpec(memory_space=pltpu.VMEM)
mesh_ids = pl.DeviceIdType.MESH


def digits(width, count, total, place):
    index = np.arange(total)
    live = index < width**count
    digit = (index // width ** (count - 1 - place)) % width
    return ((digit[None, :] == np.arange(width)[:, None]) & live[None, :]).astype(np.float32)


def others(width, count, total, place):
    index = np.arange(total)
    stride = width ** (count - 1 - place)
    rest = index - ((index // stride) % width) * stride
    return np.where(index < width**count, rest, -1).astype(np.int32)


def split(value):
    top = value.astype(jnp.bfloat16)
    return top, (value - top.astype(jnp.float32)).astype(jnp.bfloat16)


def dot3(left, right, contract):
    dims = (contract, ((), ()))
    go = functools.partial(lax.dot_general, dimension_numbers=dims, preferred_element_type=jnp.float32)
    return go(left[0], right[0]) + (go(left[0], right[1]) + go(left[1], right[0]))


def pack_kernel(plan, *refs):
    count = len(plan)
    for source, out, (rows, columns, tiles) in zip(refs[:count], refs[count:], plan):
        used = tiles * rows
        if out.shape[1] > used:
            out[:, used:, :] = jnp.zeros((out.shape[0], out.shape[1] - used, lanes), jnp.float32)
        for device in range(out.shape[0]):
            for tile in range(tiles):
                start = (device * tiles + tile) * lanes
                width = min(lanes, columns - start)
                at = slice(tile * rows, (tile + 1) * rows)
                if width < lanes:
                    out[device, at, :] = jnp.zeros((rows, lanes), jnp.float32)
                if width > 0:
                    out[device, at, :width] = source[:, start : start + width]


def build_kernel(jobs, wide, *refs):
    count = len(jobs)
    inputs, outputs = refs[:count], refs[count:-4]
    inner_over, inner_pos, full_over, full_pos = refs[-4:]
    at = 0
    layer = (lax.axis_index("grp") * lax.axis_size("sub") + lax.axis_index("sub")) // wide
    for source, (width, modes, rows, keep, lead) in zip(inputs, jobs):
        cols = source.shape[-1]
        over = [source[0, k] for k in range(modes)]
        pos = [source[1, k] for k in range(modes)]
        if keep:
            over_out, pos_out = outputs[at], outputs[at + 1]
            at += 2
        else:
            over_out, pos_out = None, outputs[at]
            at += 1
        real = width**modes
        kept = (over_out, pos_out)
        if lead:
            over_out = full_over.at[:rows, :cols] if keep else None
            pos_out = full_pos.at[:rows, :cols]
        if rows > real:
            for out in (over_out, pos_out):
                if out is not None:
                    out[real:, :] = jnp.zeros((rows - real, cols), jnp.float32)
        first, second = over[modes - 2], over[modes - 1]
        first_pos, second_pos = pos[modes - 2], pos[modes - 1]
        for a in range(width):
            span = slice(a * width, (a + 1) * width)
            over_value = first[a : a + 1] * second
            pos_value = first_pos[a : a + 1] * second + first[a : a + 1] * second_pos
            if modes == 2:
                pos_out[span, :] = pos_value
                if keep:
                    over_out[span, :] = over_value
            else:
                inner_over[span, :cols] = over_value
                inner_pos[span, :cols] = pos_value
        if modes == 3:
            square = width * width
            over_value = inner_over[:square, :cols]
            pos_value = inner_pos[:square, :cols]
            for a in range(width):
                span = slice(a * square, (a + 1) * square)
                pos_out[span, :] = pos[0][a : a + 1] * over_value + over[0][a : a + 1] * pos_value
                if keep:
                    over_out[span, :] = over[0][a : a + 1] * over_value
        if lead:
            for full, out in zip((full_over, full_pos), kept):
                if out is not None:
                    size = out.shape[0]
                    out[...] = full[pl.ds(pl.multiple_of(layer * size, 8), size), :cols]


def flow_kernel(plan, layers, wide, *refs):
    count = len(plan)
    spare = list(refs)

    def take(number):
        taken = spare[:number]
        del spare[:number]
        return taken

    sends = take(count)
    matrices = [take(len(item["targets"])) for item in plan]
    actions, rests, grams = take(count), take(count), take(count)
    gathered, mixed, back = take(count), take(count), take(count)
    value, result = take(2)
    across_send, across_recv, up_send, up_recv, down_send, down_recv, home_send, home_recv, own = spare

    sub = lax.axis_size("sub")
    me = lax.axis_index("grp") * sub + lax.axis_index("sub")
    layer, place = me // wide, me % wide

    def device(at_layer, at_place):
        index = at_layer * wide + at_place
        return (index // sub, index % sub)

    def peer(step):
        return lax.rem(place + step, wide)

    def across(t, step):
        return pltpu.make_async_remote_copy(
            src_ref=sends[t].at[peer(step)],
            dst_ref=gathered[t].at[layer, place],
            send_sem=across_send.at[t, step],
            recv_sem=across_recv.at[t, step],
            device_id=device(layer, peer(step)),
            device_id_type=mesh_ids,
        )

    def home(t, step):
        return pltpu.make_async_remote_copy(
            src_ref=mixed[t].at[peer(step)],
            dst_ref=back[t].at[place],
            send_sem=home_send.at[t, step],
            recv_sem=home_recv.at[t, step],
            device_id=device(layer, peer(step)),
            device_id_type=mesh_ids,
        )

    def hop(t, step, up):
        block = layer - step if up else layer + step
        return pltpu.make_async_remote_copy(
            src_ref=gathered[t].at[block],
            dst_ref=gathered[t].at[block],
            send_sem=(up_send if up else down_send).at[t, step],
            recv_sem=(up_recv if up else down_recv).at[t, step],
            device_id=device(layer + 1 if up else layer - 1, place),
            device_id_type=mesh_ids,
        )

    def sends_hop(step, up):
        if up:
            return jnp.logical_and(layer - step >= 0, layer + 1 < layers)
        return jnp.logical_and(layer + step < layers, layer >= 1)

    def forward(t, step):
        for up in (True, False):
            @pl.when(sends_hop(step, up))
            def _():
                hop(t, step, up).start()

    def arrive(t, step):
        @pl.when(layer - 1 - step >= 0)
        def _():
            pltpu.make_async_remote_copy(
                src_ref=gathered[t].at[layer - 1 - step],
                dst_ref=gathered[t].at[layer - 1 - step],
                send_sem=up_send.at[t, step],
                recv_sem=up_recv.at[t, step],
                device_id=device(layer - 1, place),
                device_id_type=mesh_ids,
            ).wait_recv()

        @pl.when(layer + 1 + step < layers)
        def _():
            pltpu.make_async_remote_copy(
                src_ref=gathered[t].at[layer + 1 + step],
                dst_ref=gathered[t].at[layer + 1 + step],
                send_sem=down_send.at[t, step],
                recv_sem=down_recv.at[t, step],
                device_id=device(layer + 1, place),
                device_id_type=mesh_ids,
            ).wait_recv()

    def keep(t):
        return pltpu.make_async_copy(sends[t].at[place], gathered[t].at[layer, place], own.at[t])

    def keep_home(t):
        return pltpu.make_async_copy(mixed[t].at[place], back[t].at[place], own.at[count + t])

    def layer_ready(t):
        keep(t).wait()
        for step in range(1, wide):
            across(t, step).wait_recv()

    def mix(t):
        item = plan[t]
        rows, slot, tiles = item["rows"], item["slot"], item["tiles"]
        depth = layers * wide * slot
        value[:depth, : tiles * lanes] = jnp.zeros((depth, tiles * lanes), jnp.float32)

        @pl.loop(0, layers)
        def _(at_layer):
            @pl.loop(0, wide)
            def _(at_place):
                base = pl.multiple_of((at_layer * wide + at_place) * slot, slot)
                for tile in range(tiles):
                    value[pl.ds(base, rows), tile * lanes : (tile + 1) * lanes] = gathered[t][
                        at_layer, at_place, tile * rows : (tile + 1) * rows, :
                    ]

        blocks = []
        for matrix, target in zip(matrices[t], item["targets"]):
            blocks.append(split(matrix[...]))
        mine = pl.ds(pl.multiple_of(layer * wide * slot, 8), wide * slot)
        gram = None
        for start in range(0, tiles, 2):
            wide_tiles = min(2, tiles - start)
            span = slice(start * lanes, (start + wide_tiles) * lanes)
            data = split(value[:depth, span])
            own_rows = split(value[mine, span])
            part = lax.dot_general(
                own_rows[0], data[0], (((1,), (1,)), ((), ())), preferred_element_type=jnp.float32
            ) + 2.0 * lax.dot_general(
                own_rows[0], data[1], (((1,), (1,)), ((), ())), preferred_element_type=jnp.float32
            )
            gram = part if gram is None else gram + part
            offset = 0
            for block, target in zip(blocks, item["targets"]):
                size = target * wide
                result[:size, : wide_tiles * lanes] = dot3(block, data, ((1,), (0,)))
                for at_place in range(wide):
                    for tile in range(wide_tiles):
                        row = offset + (start + tile) * target
                        mixed[t][at_place, row : row + target, :] = result[
                            at_place * target : (at_place + 1) * target, tile * lanes : (tile + 1) * lanes
                        ]
                offset += target * tiles
        if mixed[t].shape[1] > offset:
            mixed[t][:, offset:, :] = jnp.zeros((wide, mixed[t].shape[1] - offset, lanes), jnp.float32)
        grams[t][...] = gram

    def send_home(t):
        keep_home(t).start()
        for step in range(1, wide):
            home(t, step).start()

    def unpack(t):
        item = plan[t]
        tiles, columns = item["tiles"], item["columns"]
        keep_home(t).wait()
        for step in range(1, wide):
            home(t, step).wait_recv()
        offset = 0
        rest_row = 0
        for position, rows in enumerate(item["targets"]):
            for at_place in range(wide):
                for tile in range(tiles):
                    start = (at_place * tiles + tile) * lanes
                    width = min(lanes, columns - start)
                    if width > 0:
                        row = offset + tile * rows
                        got = back[t][at_place, row : row + rows, :width]
                        if position == 0:
                            actions[t][:, start : start + width] = got
                        else:
                            rests[t][rest_row : rest_row + rows, start : start + width] = got
            offset += rows * tiles
            if position:
                rest_row += rows

    barrier = pltpu.get_barrier_semaphore()
    for step in range(1, wide):
        pl.semaphore_signal(barrier, inc=1, device_id=device(layer, peer(step)), device_id_type=mesh_ids)

    @pl.when(layer + 1 < layers)
    def _():
        pl.semaphore_signal(barrier, inc=1, device_id=device(layer + 1, place), device_id_type=mesh_ids)

    @pl.when(layer >= 1)
    def _():
        pl.semaphore_signal(barrier, inc=1, device_id=device(layer - 1, place), device_id_type=mesh_ids)

    pl.semaphore_wait(barrier, wide - 1 + jnp.where(layer + 1 < layers, 1, 0) + jnp.where(layer >= 1, 1, 0))

    for t in range(count):
        keep(t).start()
        for step in range(1, wide):
            across(t, step).start()

    hops = layers - 1
    queue = []
    for t in range(count):
        for step in range(hops):
            queue.append((t, step))
    ready = set()

    def issue(t, step):
        if step == 0:
            layer_ready(t)
        else:
            arrive(t, step - 1)
        forward(t, step)
        ready.add((t, step))

    order = []
    for t in range(count):
        order.append((t, 0))
        for step in range(1, hops):
            order.append((t, step))
    for t in range(count):
        if t + 1 < count:
            ahead = (t + 1, 0)
        else:
            ahead = None
        if (t, 0) not in ready:
            issue(t, 0)
        if ahead is not None:
            issue(*ahead)
        for step in range(1, hops):
            issue(t, step)
        if hops:
            arrive(t, hops - 1)
        mix(t)
        if t:
            send_home(t - 1)
    send_home(count - 1)
    for t in range(count):
        unpack(t)

    for t in range(count):
        for step in range(1, wide):
            across(t, step).wait_send()
            home(t, step).wait_send()
        for step in range(hops):
            for up in (True, False):
                @pl.when(sends_hop(step, up))
                def _():
                    hop(t, step, up).wait_send()


def sum_kernel(layers, wide, mine, out, stage, total, send, recv):
    sub = lax.axis_size("sub")
    me = lax.axis_index("grp") * sub + lax.axis_index("sub")
    layer, place = me // wide, me % wide

    def device(at_layer, at_place):
        index = at_layer * wide + at_place
        return (index // sub, index % sub)

    barrier = pltpu.get_barrier_semaphore()
    for step in range(1, wide):
        pl.semaphore_signal(barrier, inc=1, device_id=device(layer, lax.rem(place + step, wide)), device_id_type=mesh_ids)
    for step in range(1, layers):
        pl.semaphore_signal(barrier, inc=1, device_id=device(lax.rem(layer + step, layers), place), device_id_type=mesh_ids)
    pl.semaphore_wait(barrier, wide + layers - 2)

    def first(step):
        return pltpu.make_async_remote_copy(
            src_ref=mine, dst_ref=stage.at[place], send_sem=send.at[step], recv_sem=recv.at[step],
            device_id=device(layer, lax.rem(place + step, wide)), device_id_type=mesh_ids,
        )

    def second(step):
        return pltpu.make_async_remote_copy(
            src_ref=total.at[layer], dst_ref=total.at[layer], send_sem=send.at[wide + step], recv_sem=recv.at[wide + step],
            device_id=device(lax.rem(layer + step, layers), place), device_id_type=mesh_ids,
        )

    for step in range(1, wide):
        first(step).start()
    stage[place] = mine[...]
    for step in range(1, wide):
        first(step).wait()
    total[layer] = jnp.sum(stage[...], axis=0)
    for step in range(1, layers):
        second(step).start()
    for step in range(1, layers):
        second(step).wait()
    out[...] = jnp.sum(total[...], axis=0)


def density_kernel(jobs, *refs):
    out = refs[-1]
    out[...] = jnp.zeros_like(out)
    at = 0
    for modes in jobs:
        gram = refs[at][...]
        for state_mode, width in modes:
            rest_rows, rest_columns, pick_left, pick = refs[at + 1 : at + 5]
            k = state_mode[1]
            place = state_mode[2]
            kept = jnp.where(rest_rows[:, place : place + 1] == rest_columns[place : place + 1, :], gram, 0.0)
            left = jnp.dot(pick_left[place], kept, precision=highest, preferred_element_type=jnp.float32)
            value = lax.dot_general(
                left, pick[place], (((1,), (1,)), ((), ())), precision=highest, preferred_element_type=jnp.float32
            )
            out[state_mode[0] * 8 + k, :, :] = 0.5 * (value + value.T)
        at += 5


def call(kernel, outs, scratch, *args, name, remote=None):
    extra = params
    if remote is not None:
        extra = pltpu.CompilerParams(vmem_limit_bytes=vmem_limit, collective_id=remote, has_side_effects=True)
    return pl.pallas_call(
        kernel,
        out_shape=[jax.ShapeDtypeStruct(shape, jnp.float32) for shape in outs],
        in_specs=[vmem] * len(args),
        out_specs=[vmem] * len(outs),
        scratch_shapes=[pltpu.VMEM(shape, jnp.float32) if isinstance(shape, tuple) else shape for shape in scratch],
        compiler_params=extra,
        name=name,
    )(*args)


def round_up(value, unit):
    return -(-value // unit) * unit


def spread(table, rows, slot):
    shape = table.shape[:-1]
    held = table.reshape(shape + (-1, rows))
    wider = np.full(shape + (held.shape[-2], slot), -1 if table.dtype == np.int32 else 0, table.dtype)
    wider[..., :rows] = held
    return wider.reshape(shape + (-1,))


def local(*args):
    states = args[:4]
    operators = args[4:8]
    intersections, positions, coupling_pair, coupling_mode, coupling_strength = args[8:]
    devices = lax.axis_size("grp") * lax.axis_size("sub")
    count = len(states)
    widths = [operator.shape[1] for operator in operators]
    rows = [state.shape[0] for state in states]
    columns = [state.shape[1] for state in states]
    totals = [size * devices for size in rows]
    layers = max(1, lax.axis_size("grp") // 4)
    wide = devices // layers
    layer = (lax.axis_index("grp") * lax.axis_size("sub") + lax.axis_index("sub")) // wide
    tiles = [-(-size // (wide * lanes)) for size in columns]
    slots = [round_up(size, 8) for size in rows]
    pairs, modes = intersections.shape[:2]

    sends = call(
        functools.partial(pack_kernel, [(rows[s], columns[s], tiles[s]) for s in range(count)]),
        [(wide, round_up(rows[s] * tiles[s], 8), lanes) for s in range(count)],
        [],
        *states,
        name="pack",
    )

    pair_pick = (coupling_pair[:, None] == jnp.arange(pairs, dtype=jnp.int32)[None, :]).astype(jnp.float32)
    mode_pick = (coupling_mode[:, None] == jnp.arange(modes, dtype=jnp.int32)[None, :]).astype(jnp.float32)
    weight_table = jnp.sum(
        coupling_strength[:, None, None] * pair_pick[:, :, None] * mode_pick[:, None, :], axis=0
    )
    both = jnp.stack([intersections, weight_table[:, :, None, None] * positions])

    small = {}
    for p in range(pairs):
        cut = both[:, p, :, : widths[p], : widths[p + 1]]
        small[(p, p + 1)] = cut
        small[(p + 1, p)] = jnp.swapaxes(cut, 2, 3)
    for s in range(count):
        unit = jnp.broadcast_to(jnp.eye(widths[s], dtype=jnp.float32), operators[s].shape)
        small[(s, s)] = jnp.stack([unit, operators[s]])
    jobs = []
    expanded = []
    shapes = []
    names = []
    for s, t in small:
        keep = s != t
        for part, at, span, row_total, column_total in (
            ("lead", 0, 3, totals[s], totals[t]),
            ("middle", 3, 2, widths[s] ** 2, widths[t] ** 2),
            ("tail", 5, 3, widths[s] ** 3, widths[t] ** 3),
        ):
            pick = np.stack([digits(widths[t], span, column_total, place) for place in range(span)])
            if part == "lead":
                pick = spread(pick, rows[t], slots[t])
                column_total = pick.shape[-1]
            expanded.append(
                jnp.einsum("mkab,kbc->mkac", small[(s, t)][:, at : at + span], jnp.asarray(pick), precision=highest)
            )
            jobs.append((widths[s], span, row_total, keep, part == "lead"))
            for kind in ("over", "pos") if keep else ("pos",):
                shapes.append((row_total // layers if part == "lead" else row_total, column_total))
                names.append((s, t, part, kind))
    widest = round_up(max(devices * max(slots), max(widths) ** 3), lanes)
    built = call(
        functools.partial(build_kernel, jobs, wide),
        shapes,
        [(round_up(max(widths) ** 2, 8), widest)] * 2 + [(max(totals), widest)] * 2,
        *expanded,
        name="build",
    )
    matrices = dict(zip(names, built))

    order = [[(t, "pos")] + [(s, kind) for s in (t - 1, t + 1) if 0 <= s < count for kind in ("over", "pos")] for t in range(count)]
    plan = [
        dict(rows=rows[t], slot=slots[t], tiles=tiles[t], columns=columns[t], targets=[rows[s] for s, kind in order[t]])
        for t in range(count)
    ]
    back_shapes = [(wide, round_up(sum(item["targets"]) * item["tiles"], 8), lanes) for item in plan]
    rest_rows = [sum(rows[s] for s, kind in order[t][1:]) for t in range(count)]
    dma = pltpu.SemaphoreType.DMA
    flowed = call(
        functools.partial(flow_kernel, plan, layers, wide),
        [(rows[t], columns[t]) for t in range(count)]
        + [(rest_rows[t], columns[t]) for t in range(count)]
        + [(wide * slots[t], devices * slots[t]) for t in range(count)],
        [(layers,) + send.shape for send in sends]
        + back_shapes * 2
        + [
            (devices * max(slots), max(tiles) * lanes),
            (wide * max(rows), 2 * lanes),
            dma((count, wide)),
            dma((count, wide)),
            dma((count, layers)),
            dma((count, layers)),
            dma((count, layers)),
            dma((count, layers)),
            dma((count, wide)),
            dma((count, wide)),
            dma((2 * count,)),
        ],
        *sends,
        *[matrices[(s, t, "lead", kind)] for t in range(count) for s, kind in order[t]],
        name="flow",
        remote=0,
    )
    actions, rests, grams = flowed[:count], flowed[count : 2 * count], flowed[2 * count :]

    cubes = [states[t].reshape(rows[t], widths[t] ** 2, widths[t] ** 3) for t in range(count)]
    density_jobs = []
    density_args = []
    for t in range(count):
        middle = jnp.einsum("rqc,rpc->qp", cubes[t], cubes[t], precision=high)
        tail = jnp.einsum("rqc,rqd->cd", cubes[t], cubes[t], precision=high)
        for gram, at, span in ((grams[t], 0, 3), (middle, 3, 2), (tail, 5, 3)):
            size = totals[t] if at == 0 else gram.shape[0]
            rest = np.stack([others(widths[t], span, size, place) for place in range(span)])
            pick = np.zeros((span, 8, size), np.float32)
            for place in range(span):
                pick[place, : widths[t]] = digits(widths[t], span, size, place)
            if at == 0:
                rest, pick = spread(rest, rows[t], slots[t]), spread(pick, rows[t], slots[t])
            rest_left, pick_left = rest.T, pick
            if at == 0:
                size = wide * slots[t]
                rest_left = lax.dynamic_slice_in_dim(jnp.asarray(rest.T), layer * size, size, 0)
                pick_left = lax.dynamic_slice_in_dim(jnp.asarray(pick), layer * size, size, 2)
            density_jobs.append([((t, at + place, place), widths[t]) for place in range(span)])
            density_args += [gram] + [jnp.asarray(item) for item in (rest_left, rest, pick_left, pick)]
    (blocks,) = call(
        functools.partial(density_kernel, density_jobs), [(count * 8, 8, 8)], [], *density_args, name="density"
    )
    shape = (blocks.size // lanes, lanes)
    (summed,) = call(
        functools.partial(sum_kernel, layers, wide),
        [shape],
        [(wide,) + shape, (layers,) + shape, dma((wide + layers,)), dma((wide + layers,))],
        blocks.reshape(shape),
        name="sum",
        remote=1,
    )
    summed = summed.reshape(blocks.shape)
    densities = [
        summed[t * 8 : t * 8 + modes, : widths[t], : widths[t]] / float(widths[t] ** (modes - 1)) for t in range(count)
    ]

    right = functools.partial(jnp.einsum, "rqc,dc->rqd", precision=high)
    left = functools.partial(jnp.einsum, "aq,rqd->rad", precision=high)
    total = []
    for t in range(count):
        total.append(right(cubes[t], matrices[(t, t, "tail", "pos")]) + left(matrices[(t, t, "middle", "pos")], cubes[t]))
    for t in range(count):
        rest = rests[t].reshape(rest_rows[t], widths[t] ** 2, widths[t] ** 3)
        start = 0
        for s in (t - 1, t + 1):
            if not 0 <= s < count:
                continue
            over_rows = rest[start : start + rows[s]]
            pos_rows = rest[start + rows[s] : start + 2 * rows[s]]
            start += 2 * rows[s]
            over_tail, pos_tail = matrices[(s, t, "tail", "over")], matrices[(s, t, "tail", "pos")]
            once = right(pos_rows, over_tail) + right(over_rows, pos_tail)
            twice = right(over_rows, over_tail)
            total[s] = (
                total[s]
                + left(matrices[(s, t, "middle", "over")], once)
                + left(matrices[(s, t, "middle", "pos")], twice)
            )
    stepped = [
        states[s] - time_step * (total[s].reshape(rows[s], columns[s]) + actions[s]) for s in range(count)
    ]
    return tuple(stepped) + tuple(densities)


def solution(mesh):
    spread = P(("grp", "sub"), None)
    return jax.shard_map(
        local,
        mesh=mesh,
        in_specs=(spread,) * 4 + (P(),) * 9,
        out_specs=(spread,) * 4 + (P(),) * 4,
        check_vma=False,
    )
```

```python
import functools
import math

import jax
import jax.numpy as jnp
import numpy as np
from jax import lax
from jax.experimental import pallas as pl
from jax.experimental.pallas import tpu as pltpu
from jax.sharding import PartitionSpec as P

highest = lax.Precision.HIGHEST
time_step = 0.25
lanes = 128
vmem_limit = 63 * 1024 * 1024
params = pltpu.CompilerParams(vmem_limit_bytes=vmem_limit)
vmem = pl.BlockSpec(memory_space=pltpu.VMEM)
mesh_ids = pl.DeviceIdType.MESH


def digits(width, count, total, place):
    index = np.arange(total)
    live = index < width**count
    digit = (index // width ** (count - 1 - place)) % width
    return ((digit[None, :] == np.arange(width)[:, None]) & live[None, :]).astype(np.float32)


def others(width, count, total, place):
    index = np.arange(total)
    stride = width ** (count - 1 - place)
    rest = index - ((index // stride) % width) * stride
    return np.where(index < width**count, rest, -1).astype(np.int32)


def split(value):
    top = value.astype(jnp.bfloat16)
    return top, (value - top.astype(jnp.float32)).astype(jnp.bfloat16)


def dot3(left, right, contract):
    dims = (contract, ((), ()))
    go = functools.partial(lax.dot_general, dimension_numbers=dims, preferred_element_type=jnp.float32)
    return go(left[0], right[0]) + (go(left[0], right[1]) + go(left[1], right[0]))


def pack_kernel(plan, *refs):
    count = len(plan)
    for source, out, (rows, columns, tiles) in zip(refs[:count], refs[count:], plan):
        used = tiles * rows
        if out.shape[1] > used:
            out[:, used:, :] = jnp.zeros((out.shape[0], out.shape[1] - used, lanes), jnp.float32)
        for device in range(out.shape[0]):
            for tile in range(tiles):
                start = (device * tiles + tile) * lanes
                width = min(lanes, columns - start)
                at = slice(tile * rows, (tile + 1) * rows)
                if width < lanes:
                    out[device, at, :] = jnp.zeros((rows, lanes), jnp.float32)
                if width > 0:
                    out[device, at, :width] = source[:, start : start + width]


def flow_kernel(plan, combos, layers, wide, *refs):
    count = len(plan)
    spare = list(refs)

    def take(number):
        taken = spare[:number]
        del spare[:number]
        return taken

    sends, states = take(count), take(count)
    small, scalars = take(2)
    kinds = [item["kind"] for item in plan]
    tables = [take(max(kinds) + 1) for _ in range(8)]
    lead_pick, lead_turned, lead_rest, lead_rest_turned, tail_pick, tail_turned, tail_rest, tail_rest_turned = [
        [table[kind] for kind in kinds] for table in tables
    ]
    stepped, densities = take(count), take(count)
    gathered, mixed, back = take(count), take(count), take(count)
    value, result = take(2)
    matrices = [take(len(item["targets"])) for item in plan]
    tails = {key: take(1 if key[0] == key[1] else 2) for key in combos}
    cubes, totals = take(count), take(count)
    zero_in, one_in, zero_out, one_out = take(4)
    inner_over, inner_pos, full_over, full_pos = take(4)
    sums, stage, layer_sums, rows_of_sums = take(4)
    across_send, across_recv, up_send, up_recv, down_send, down_recv, home_send, home_recv, own, sum_send, sum_recv = spare

    sub = lax.axis_size("sub")
    me = lax.axis_index("grp") * sub + lax.axis_index("sub")
    layer, place = me // wide, me % wide

    def device(at_layer, at_place):
        index = at_layer * wide + at_place
        return (index // sub, index % sub)

    def peer(step):
        return lax.rem(place + step, wide)

    def across(t, step):
        return pltpu.make_async_remote_copy(
            src_ref=sends[t].at[peer(step)],
            dst_ref=gathered[t].at[layer, place],
            send_sem=across_send.at[t, step],
            recv_sem=across_recv.at[t, step],
            device_id=device(layer, peer(step)),
            device_id_type=mesh_ids,
        )

    def home(t, step):
        return pltpu.make_async_remote_copy(
            src_ref=mixed[t].at[peer(step)],
            dst_ref=back[t].at[place],
            send_sem=home_send.at[t, step],
            recv_sem=home_recv.at[t, step],
            device_id=device(layer, peer(step)),
            device_id_type=mesh_ids,
        )

    def hop(t, step, up):
        block = layer - step if up else layer + step
        return pltpu.make_async_remote_copy(
            src_ref=gathered[t].at[block],
            dst_ref=gathered[t].at[block],
            send_sem=(up_send if up else down_send).at[t, step],
            recv_sem=(up_recv if up else down_recv).at[t, step],
            device_id=device(layer + 1 if up else layer - 1, place),
            device_id_type=mesh_ids,
        )

    def sends_hop(step, up):
        if up:
            return jnp.logical_and(layer - step >= 0, layer + 1 < layers)
        return jnp.logical_and(layer + step < layers, layer >= 1)

    def forward(t, step):
        for up in (True, False):
            @pl.when(sends_hop(step, up))
            def _():
                hop(t, step, up).start()

    def arrive(t, step):
        @pl.when(layer - 1 - step >= 0)
        def _():
            pltpu.make_async_remote_copy(
                src_ref=gathered[t].at[layer - 1 - step],
                dst_ref=gathered[t].at[layer - 1 - step],
                send_sem=up_send.at[t, step],
                recv_sem=up_recv.at[t, step],
                device_id=device(layer - 1, place),
                device_id_type=mesh_ids,
            ).wait_recv()

        @pl.when(layer + 1 + step < layers)
        def _():
            pltpu.make_async_remote_copy(
                src_ref=gathered[t].at[layer + 1 + step],
                dst_ref=gathered[t].at[layer + 1 + step],
                send_sem=down_send.at[t, step],
                recv_sem=down_recv.at[t, step],
                device_id=device(layer + 1, place),
                device_id_type=mesh_ids,
            ).wait_recv()

    def keep(t):
        return pltpu.make_async_copy(sends[t].at[place], gathered[t].at[layer, place], own.at[t])

    def keep_home(t):
        return pltpu.make_async_copy(mixed[t].at[place], back[t].at[place], own.at[count + t])

    def layer_ready(t):
        keep(t).wait()
        for step in range(1, wide):
            across(t, step).wait_recv()

    def put_density(t, mode, block):
        at = (t * 8 + mode) * 8
        sums[:, at : at + 8] = block

    def add_density(t, mode, gram, rest_rows, rest_columns, pick, turned):
        kept = split(jnp.where(rest_rows == rest_columns, gram, 0.0))
        chosen = pick.astype(jnp.bfloat16)
        dims = (((1,), (1,)), ((), ()))
        right = lax.dot_general(kept[0], chosen, dims, preferred_element_type=jnp.float32) + lax.dot_general(
            kept[1], chosen, dims, preferred_element_type=jnp.float32
        )
        block = lax.dot_general(
            turned, right, (((0,), (0,)), ((), ())), precision=highest, preferred_element_type=jnp.float32
        )
        put_density(t, mode, 0.5 * (block + block.T))

    def mix(t):
        item = plan[t]
        rows, slot, tiles = item["rows"], item["slot"], item["tiles"]
        depth = layers * wide * slot
        value[:depth, : tiles * lanes] = jnp.zeros((depth, tiles * lanes), jnp.float32)

        @pl.loop(0, layers)
        def _(at_layer):
            @pl.loop(0, wide)
            def _(at_place):
                base = pl.multiple_of((at_layer * wide + at_place) * slot, slot)
                for tile in range(tiles):
                    value[pl.ds(base, rows), tile * lanes : (tile + 1) * lanes] = gathered[t][
                        at_layer, at_place, tile * rows : (tile + 1) * rows, :
                    ]

        blocks = []
        for matrix in matrices[t]:
            blocks.append(split(matrix[...]))
        mine = pl.ds(pl.multiple_of(layer * wide * slot, 8), wide * slot)
        gram = None
        for start in range(0, tiles, 2):
            wide_tiles = min(2, tiles - start)
            span = slice(start * lanes, (start + wide_tiles) * lanes)
            data = split(value[:depth, span])
            own_rows = split(value[mine, span])
            part = lax.dot_general(
                own_rows[0], data[0], (((1,), (1,)), ((), ())), preferred_element_type=jnp.float32
            ) + 2.0 * lax.dot_general(
                own_rows[0], data[1], (((1,), (1,)), ((), ())), preferred_element_type=jnp.float32
            )
            gram = part if gram is None else gram + part
            offset = 0
            for block, target in zip(blocks, item["targets"]):
                size = target * wide
                result[:size, : wide_tiles * lanes] = dot3(block, data, ((1,), (0,)))
                for at_place in range(wide):
                    for tile in range(wide_tiles):
                        row = offset + (start + tile) * target
                        mixed[t][at_place, row : row + target, :] = result[
                            at_place * target : (at_place + 1) * target, tile * lanes : (tile + 1) * lanes
                        ]
                offset += target * tiles
        if mixed[t].shape[1] > offset:
            mixed[t][:, offset:, :] = jnp.zeros((wide, mixed[t].shape[1] - offset, lanes), jnp.float32)
        for k in range(3):
            turned = lead_turned[t][k, mine, :]
            add_density(t, k, gram, lead_rest_turned[t][mine, k : k + 1], lead_rest[t][k : k + 1, :], lead_pick[t][k], turned)

    def send_home(t):
        keep_home(t).start()
        for step in range(1, wide):
            home(t, step).start()

    def expand(key, kind, mode, pick):
        matrix = small[(combos[key] * 2 + kind) * 8 + mode]
        out = None
        for b in range(plan[key[1]]["width"]):
            term = matrix[:, b : b + 1] * pick[b : b + 1, :]
            out = term if out is None else out + term
        return out

    def build(key, picks, mode, over_out, pos_out, rows):
        width = plan[key[0]]["width"]
        cols = picks.shape[-1]
        over = [expand(key, 0, mode + k, picks[k]) for k in range(3)]
        pos = [expand(key, 1, mode + k, picks[k]) for k in range(3)]
        square = width * width
        if rows > square * width:
            for out in (over_out, pos_out):
                if out is not None:
                    out[square * width : rows, :cols] = jnp.zeros((rows - square * width, cols), jnp.float32)
        for a in range(width):
            span = slice(a * width, (a + 1) * width)
            inner_over[span, :cols] = over[1][a : a + 1] * over[2][:width]
            inner_pos[span, :cols] = pos[1][a : a + 1] * over[2][:width] + over[1][a : a + 1] * pos[2][:width]
        over_value = inner_over[:square, :cols]
        pos_value = inner_pos[:square, :cols]
        for a in range(width):
            span = slice(a * square, (a + 1) * square)
            pos_out[span, :cols] = pos[0][a : a + 1] * over_value + over[0][a : a + 1] * pos_value
            if over_out is not None:
                over_out[span, :cols] = over[0][a : a + 1] * over_value

    def build_leads(t):
        cols = plan[t]["slot"] * layers * wide
        sources = [t] + [s for s in (t - 1, t + 1) if 0 <= s < count]
        at = 0
        for s in sources:
            rows = plan[s]["rows"]
            build((s, t), lead_pick[t], 0, full_over if s != t else None, full_pos, rows * layers * wide)
            mine = pl.ds(pl.multiple_of(layer * rows * wide, 8), rows * wide)
            for full in (full_over, full_pos) if s != t else (full_pos,):
                matrices[t][at][...] = full[mine, :cols]
                at += 1

    def build_tail(s, t):
        outs = tails[(s, t)]
        build((t, s), tail_pick[s], 5, outs[0] if s != t else None, outs[-1], plan[t]["width"] ** 3)

    def cube(s):
        item = plan[s]
        rows, slot, width = item["rows"], item["slot"], item["width"]
        size = width**3
        cubes[s][...] = jnp.zeros(cubes[s].shape, jnp.float32)
        for q in range(width**2):
            cubes[s][q * slot : q * slot + rows, :size] = states[s][:, q * size : (q + 1) * size]

    def scalar(key, kind, mode, a, b):
        return scalars[((combos[key] * 2 + kind) * 2 + mode) * 64 + a * 8 + b]

    def self_part(s):
        item = plan[s]
        slot, width = item["slot"], item["width"]
        size = width**3
        total = totals[s]
        total[:, :size] = dot3(split(cubes[s][:, :size]), split(tails[(s, s)][0][:, :size]), ((1,), (0,)))
        block = width * slot
        for tile in range(-(-size // lanes)):
            at = slice(tile * lanes, (tile + 1) * lanes)

            @pl.loop(0, width)
            def _(i):
                base = pl.multiple_of(i * block, 8)
                held = [cubes[s][pl.ds(base + b * slot, slot), at] for b in range(width)]
                for a in range(width):
                    out = total[pl.ds(base + a * slot, slot), at]
                    for b in range(width):
                        out = out + scalar((s, s), 1, 1, a, b) * held[b]
                    total[pl.ds(base + a * slot, slot), at] = out

            @pl.loop(0, width)
            def _(i):
                base = pl.multiple_of(i * slot, 8)
                held = [cubes[s][pl.ds(base + b * block, slot), at] for b in range(width)]
                for a in range(width):
                    out = total[pl.ds(base + a * block, slot), at]
                    for b in range(width):
                        out = out + scalar((s, s), 1, 0, a, b) * held[b]
                    total[pl.ds(base + a * block, slot), at] = out

    def self_density(s):
        item = plan[s]
        slot, width = item["slot"], item["width"]
        size = width**3
        data = split(cubes[s][:, :size])
        gram = None
        step = width * slot
        dims = (((0,), (0,)), ((), ()))
        gram = lax.dot_general(data[0], data[0], dims, preferred_element_type=jnp.float32) + 2.0 * lax.dot_general(
            data[0], data[1], dims, preferred_element_type=jnp.float32
        )
        for k in range(3):
            add_density(
                s, 5 + k, gram, tail_rest_turned[s][:, k : k + 1], tail_rest[s][k : k + 1, :], tail_pick[s][k], tail_turned[s][k]
            )
        column = lax.broadcasted_iota(jnp.int32, (8, 8), 1)
        wide_lanes = cubes[s].shape[1]
        rows_of_sums[...] = jnp.zeros(rows_of_sums.shape, jnp.float32)
        for mode in range(2):
            block = jnp.zeros((8, 8), jnp.float32)
            for i in range(width):
                for j in range(width):
                    row = None
                    for other in range(width):
                        left = (i * width + other if mode == 0 else other * width + i) * slot
                        right = (j * width + other if mode == 0 else other * width + j) * slot
                        term = cubes[s][left : left + slot, :] * cubes[s][right : right + slot, :]
                        row = term if row is None else row + term
                    rows_of_sums[j : j + 1, :wide_lanes] = jnp.sum(row, axis=0, keepdims=True)
                column_sum = jnp.sum(rows_of_sums[:, :wide_lanes], axis=1, keepdims=True)
                block = jnp.where(column == i, column_sum, block)
            put_density(s, 3 + mode, block)

    def pieces(t):
        item = plan[t]
        tiles, columns, size = item["tiles"], item["columns"], item["width"] ** 3
        out = []
        for at_place in range(wide):
            for tile in range(tiles):
                start = (at_place * tiles + tile) * lanes
                stop = min(start + lanes, columns)
                while start < stop:
                    q = start // size
                    end = min(stop, (q + 1) * size)
                    out.append((at_place, tile, start % lanes, end - start, q, start - q * size, start))
                    start = end
        return out

    def wait_home(t):
        keep_home(t).wait()
        for step in range(1, wide):
            home(t, step).wait_recv()

    def take_action(t):
        item = plan[t]
        rows, tiles = item["rows"], item["tiles"]
        for at_place in range(wide):
            for tile in range(tiles):
                start = (at_place * tiles + tile) * lanes
                width = min(lanes, item["columns"] - start)
                if width > 0:
                    stepped[t][:, start : start + width] = back[t][at_place, tile * rows : (tile + 1) * rows, :width]

    def pair_part(s, t):
        item = plan[t]
        rows, slot = plan[s]["rows"], plan[s]["slot"]
        wide_in, wide_out, size = item["width"], plan[s]["width"], item["width"] ** 3
        offset = item["rows"] * item["tiles"]
        if s > t and t > 0:
            offset += 2 * plan[t - 1]["rows"] * item["tiles"]
        listed = pieces(t)
        for target in (zero_in, one_in):
            for at_place, tile, lane, length, q, inside, _ in listed:
                row = offset + tile * rows
                target[q * slot : q * slot + rows, inside : inside + length] = back[t][
                    at_place, row : row + rows, lane : lane + length
                ]
            offset += rows * item["tiles"]

        def stage_of(mode, loops, step, in_stride, out_stride, out_step, zero_from, one_from, zero_to, one_to):
            for tile in range(-(-size // lanes)):
                at = slice(tile * lanes, (tile + 1) * lanes)

                @pl.loop(0, loops)
                def _(i):
                    base = pl.multiple_of(i * step, 8)
                    out_base = pl.multiple_of(i * out_step, 8)
                    for group in range(0, slot, 8):
                        zero = [zero_from[pl.ds(base + b * in_stride + group, 8), at] for b in range(wide_in)]
                        one = [one_from[pl.ds(base + b * in_stride + group, 8), at] for b in range(wide_in)]
                        for a in range(wide_out):
                            next_zero, next_one = None, None
                            for b in range(wide_in):
                                over, pos = scalar((s, t), 0, mode, a, b), scalar((s, t), 1, mode, a, b)
                                zero_term, one_term = over * zero[b], over * one[b] + pos * zero[b]
                                next_zero = zero_term if b == 0 else next_zero + zero_term
                                next_one = one_term if b == 0 else next_one + one_term
                            zero_to[pl.ds(out_base + a * out_stride + group, 8), at] = next_zero
                            one_to[pl.ds(out_base + a * out_stride + group, 8), at] = next_one

        stage_of(1, wide_in, wide_in * slot, slot, slot, wide_out * slot, zero_in, one_in, zero_out, one_out)
        stage_of(0, wide_out, slot, wide_out * slot, wide_out * slot, slot, zero_out, one_out, zero_in, one_in)
        live = wide_out**2 * slot
        out_size = wide_out**3
        over_tail, pos_tail = tails[(s, t)]
        totals[s][:, :out_size] += dot3(
            split(one_in[:live, :size]), split(over_tail[:, :out_size]), ((1,), (0,))
        ) + dot3(split(zero_in[:live, :size]), split(pos_tail[:, :out_size]), ((1,), (0,)))

    def finish(s):
        item = plan[s]
        rows, slot, size = item["rows"], item["slot"], item["width"] ** 3
        for q in range(item["width"] ** 2):
            at = slice(q * size, (q + 1) * size)
            stepped[s][:, at] = states[s][:, at] - time_step * (
                totals[s][q * slot : q * slot + rows, :size] + stepped[s][:, at]
            )

    def first_sum(step):
        return pltpu.make_async_remote_copy(
            src_ref=sums,
            dst_ref=stage.at[place],
            send_sem=sum_send.at[step],
            recv_sem=sum_recv.at[step],
            device_id=device(layer, peer(step)),
            device_id_type=mesh_ids,
        )

    def second_sum(step):
        return pltpu.make_async_remote_copy(
            src_ref=layer_sums.at[layer],
            dst_ref=layer_sums.at[layer],
            send_sem=sum_send.at[wide + step],
            recv_sem=sum_recv.at[wide + step],
            device_id=device(lax.rem(layer + step, layers), place),
            device_id_type=mesh_ids,
        )

    barrier = pltpu.get_barrier_semaphore()
    for step in range(1, wide):
        pl.semaphore_signal(barrier, inc=1, device_id=device(layer, peer(step)), device_id_type=mesh_ids)
    for step in range(1, layers):
        pl.semaphore_signal(
            barrier, inc=1, device_id=device(lax.rem(layer + step, layers), place), device_id_type=mesh_ids
        )
    pl.semaphore_wait(barrier, wide + layers - 2)

    hops = layers - 1
    early, late = 1, 0
    others = [t for t in range(count) if t not in (early, late)]
    for t in [early, late] + others:
        keep(t).start()
        for step in range(1, wide):
            across(t, step).start()

    def begin(t):
        layer_ready(t)
        forward(t, 0)

    def relay(t, step):
        arrive(t, step - 1)
        forward(t, step)

    begin(early)
    build_leads(early)
    for step in range(1, min(2, hops)):
        relay(early, step)
    begin(late)
    for step in range(2, hops):
        relay(early, step)
    for t in [late] + others:
        build_leads(t)
    arrive(early, hops - 1)
    mix(early)
    for t in others:
        begin(t)
    send_home(early)
    for s in range(count):
        cube(s)
        build_tail(s, s)
    relay(late, 1)
    for s in range(count):
        for t in (s - 1, s + 1):
            if 0 <= t < count:
                build_tail(s, t)
    for s in range(count):
        self_part(s)
    wait_home(early)
    take_action(early)
    pair_part(0, early)
    for step in range(2, hops):
        relay(late, step)
    for t in others:
        relay(t, 1)
    pair_part(2, early)
    for s in range(count):
        self_density(s)
    for t in others:
        for step in range(2, hops):
            relay(t, step)
    arrive(late, hops - 1)
    mix(late)
    last = late
    for t in others:
        arrive(t, hops - 1)
        mix(t)
        send_home(last)
        last = t
    for step in range(1, wide):
        first_sum(step).start()
    stage[place] = sums[...]
    send_home(last)
    for t in [late] + others:
        wait_home(t)
        take_action(t)
        for s in (t - 1, t + 1):
            if 0 <= s < count:
                pair_part(s, t)
        if t == late:
            for step in range(1, wide):
                first_sum(step).wait()
            layer_sums[layer] = jnp.sum(stage[...], axis=0)
        if t == others[0]:
            for step in range(1, layers):
                second_sum(step).start()
    for s in range(count):
        finish(s)
    for step in range(1, layers):
        second_sum(step).wait()
    whole = jnp.sum(layer_sums[...], axis=0)
    for t in range(count):
        width = plan[t]["width"]
        for mode in range(8):
            at = (t * 8 + mode) * 8
            densities[t][mode] = whole[:width, at : at + width] * (1.0 / float(width**7))

    for t in range(count):
        for step in range(1, wide):
            across(t, step).wait_send()
            home(t, step).wait_send()
        for step in range(hops):
            for up in (True, False):
                @pl.when(sends_hop(step, up))
                def _():
                    hop(t, step, up).wait_send()


def call(kernel, outs, scratch, *args, name, remote=None):
    extra = params
    if remote is not None:
        extra = pltpu.CompilerParams(vmem_limit_bytes=vmem_limit, collective_id=remote, has_side_effects=True)
    return pl.pallas_call(
        kernel,
        out_shape=[jax.ShapeDtypeStruct(shape, jnp.float32) for shape in outs],
        in_specs=[pl.BlockSpec(memory_space=pltpu.SMEM) if arg.ndim == 1 else vmem for arg in args],
        out_specs=[vmem] * len(outs),
        scratch_shapes=[pltpu.VMEM(shape, jnp.float32) if isinstance(shape, tuple) else shape for shape in scratch],
        compiler_params=extra,
        name=name,
    )(*args)


def round_up(value, unit):
    return -(-value // unit) * unit


def spread(table, rows, slot):
    shape = table.shape[:-1]
    held = table.reshape(shape + (-1, rows))
    wider = np.full(shape + (held.shape[-2], slot), -1 if table.dtype == np.int32 else 0, table.dtype)
    wider[..., :rows] = held
    return wider.reshape(shape + (-1,))


def local(*args):
    states = args[:4]
    operators = args[4:8]
    intersections, positions, coupling_pair, coupling_mode, coupling_strength = args[8:]
    devices = lax.axis_size("grp") * lax.axis_size("sub")
    count = len(states)
    widths = [operator.shape[1] for operator in operators]
    rows = [state.shape[0] for state in states]
    columns = [state.shape[1] for state in states]
    totals = [size * devices for size in rows]
    layers = max(1, lax.axis_size("grp") // 4)
    wide = devices // layers
    tiles = [-(-size // (wide * lanes)) for size in columns]
    slots = [round_up(size, 8) for size in rows]
    pairs, modes = intersections.shape[:2]

    sends = call(
        functools.partial(pack_kernel, [(rows[s], columns[s], tiles[s]) for s in range(count)]),
        [(wide, round_up(rows[s] * tiles[s], 8), lanes) for s in range(count)],
        [],
        *states,
        name="pack",
    )

    pair_pick = (coupling_pair[:, None] == jnp.arange(pairs, dtype=jnp.int32)[None, :]).astype(jnp.float32)
    mode_pick = (coupling_mode[:, None] == jnp.arange(modes, dtype=jnp.int32)[None, :]).astype(jnp.float32)
    weight_table = jnp.sum(
        coupling_strength[:, None, None] * pair_pick[:, :, None] * mode_pick[:, None, :], axis=0
    )
    both = jnp.stack([intersections, weight_table[:, :, None, None] * positions])

    def square(cut):
        return jnp.pad(cut, ((0, 0), (0, 0), (0, 8 - cut.shape[2]), (0, 8 - cut.shape[3])))

    combos = {}
    small = []
    for p in range(pairs):
        cut = both[:, p, :, : widths[p], : widths[p + 1]]
        for key, item in (((p, p + 1), cut), ((p + 1, p), jnp.swapaxes(cut, 2, 3))):
            combos[key] = len(small)
            small.append(square(item))
    for s in range(count):
        unit = jnp.broadcast_to(jnp.eye(widths[s], dtype=jnp.float32), operators[s].shape)
        turned = jnp.concatenate([operators[s][:5], jnp.swapaxes(operators[s][5:], 1, 2)])
        combos[(s, s)] = len(small)
        small.append(square(jnp.stack([unit, turned])))
    small = jnp.stack(small)
    scalars = small[:, :, 3:5].reshape(-1)
    small = small.reshape(-1, 8, 8)

    order = [[(t, "pos")] + [(s, kind) for s in (t - 1, t + 1) if 0 <= s < count for kind in ("over", "pos")] for t in range(count)]
    kinds = list(dict.fromkeys(zip(widths, rows)))
    plan = [
        dict(
            rows=rows[t],
            slot=slots[t],
            tiles=tiles[t],
            columns=columns[t],
            width=widths[t],
            kind=kinds.index((widths[t], rows[t])),
            targets=[rows[s] for s, kind in order[t]],
        )
        for t in range(count)
    ]
    back_shapes = [(wide, round_up(sum(item["targets"]) * item["tiles"], 8), lanes) for item in plan]
    tables = {name: [] for name in ("pick", "turned", "rest", "rest_turned")}
    for lead in (True, False):
        for width, held in kinds:
            size = held * devices if lead else width**3
            pick = np.zeros((3, 8, size), np.float32)
            rest = np.stack([others(width, 3, size, place) for place in range(3)])
            for place in range(3):
                pick[place, :width] = digits(width, 3, size, place)
            if lead:
                rest, pick = spread(rest, held, round_up(held, 8)), spread(pick, held, round_up(held, 8))
            tables["pick"].append(jnp.asarray(pick))
            tables["turned"].append(jnp.asarray(np.ascontiguousarray(pick.transpose(0, 2, 1))))
            tables["rest"].append(jnp.asarray(rest))
            tables["rest_turned"].append(jnp.asarray(np.ascontiguousarray(rest.T)))
    names = ("pick", "turned", "rest", "rest_turned")
    constants = [item for name in names for item in tables[name][: len(kinds)]] + [
        item for name in names for item in tables[name][len(kinds) :]
    ]
    cube_shapes = [(widths[s] ** 2 * slots[s], round_up(widths[s] ** 3, lanes)) for s in range(count)]
    mixed_shape = (max(widths) ** 2 * max(slots), round_up(max(widths) ** 3, lanes))
    depths = [devices * slots[t] for t in range(count)]
    dma = pltpu.SemaphoreType.DMA
    sum_shape = (8, count * 64)
    flowed = call(
        functools.partial(flow_kernel, plan, combos, layers, wide),
        [state.shape for state in states] + [(modes, widths[t], widths[t]) for t in range(count)],
        [(layers,) + send.shape for send in sends]
        + back_shapes * 2
        + [(max(depths), max(tiles) * lanes), (wide * max(rows), 2 * lanes)]
        + [(wide * rows[s], depths[t]) for t in range(count) for s, kind in order[t]]
        + [(widths[t] ** 3, round_up(widths[s] ** 3, lanes)) for s, t in combos for _ in range(1 if s == t else 2)]
        + cube_shapes * 2
        + [mixed_shape] * 4
        + [(round_up(max(widths) ** 2, 8), max(depths + [mixed_shape[1]]))] * 2
        + [(max(totals), max(depths))] * 2
        + [sum_shape, (wide,) + sum_shape, (layers,) + sum_shape, (8, mixed_shape[1])]
        + [dma((count, wide))] * 2
        + [dma((count, layers))] * 4
        + [dma((count, wide))] * 2
        + [dma((2 * count,))]
        + [dma((wide + layers,))] * 2,
        *sends,
        *states,
        small,
        scalars,
        *constants,
        name="flow",
        remote=0,
    )
    return tuple(flowed)


def solution(mesh):
    sharded = P(("grp", "sub"), None)
    return jax.shard_map(
        local,
        mesh=mesh,
        in_specs=(sharded,) * 4 + (P(),) * 9,
        out_specs=(sharded,) * 4 + (P(),) * 4,
        check_vma=False,
    )
```

```python
import functools
import math

import jax
import jax.numpy as jnp
import numpy as np
from jax import lax
from jax.experimental import pallas as pl
from jax.experimental.pallas import tpu as pltpu
from jax.sharding import PartitionSpec as P

highest = lax.Precision.HIGHEST
time_step = 0.25
lanes = 128
vmem_limit = 63 * 1024 * 1024
params = pltpu.CompilerParams(vmem_limit_bytes=vmem_limit)
vmem = pl.BlockSpec(memory_space=pltpu.VMEM)
mesh_ids = pl.DeviceIdType.MESH


def digits(width, count, total, place):
    index = np.arange(total)
    live = index < width**count
    digit = (index // width ** (count - 1 - place)) % width
    return ((digit[None, :] == np.arange(width)[:, None]) & live[None, :]).astype(np.float32)


def others(width, count, total, place):
    index = np.arange(total)
    stride = width ** (count - 1 - place)
    rest = index - ((index // stride) % width) * stride
    return np.where(index < width**count, rest, -1).astype(np.int32)


def split(value):
    top = value.astype(jnp.bfloat16)
    return top, (value - top.astype(jnp.float32)).astype(jnp.bfloat16)


def dot3(left, right, contract):
    dims = (contract, ((), ()))
    go = functools.partial(lax.dot_general, dimension_numbers=dims, preferred_element_type=jnp.float32)
    return go(left[0], right[0]) + (go(left[0], right[1]) + go(left[1], right[0]))


def pack_kernel(plan, chunks, *refs):
    count = len(plan)
    sources = refs[:count]
    for out, (t, first, number) in zip(refs[count:], chunks):
        source, item = sources[t], plan[t]
        rows = item["rows"]
        used = number * rows
        if out.shape[1] > used:
            out[:, used:, :] = jnp.zeros((out.shape[0], out.shape[1] - used, lanes), jnp.float32)
        for device in range(out.shape[0]):
            for tile in range(number):
                start = (device * item["tiles"] + first + tile) * lanes
                width = min(lanes, item["columns"] - start)
                at = slice(tile * rows, (tile + 1) * rows)
                if width < lanes:
                    out[device, at, :] = jnp.zeros((rows, lanes), jnp.float32)
                if width > 0:
                    out[device, at, :width] = source[:, start : start + width]


def finish_kernel(count, *refs):
    states, changes, sums = refs[:count], refs[count : 2 * count], refs[2 * count]
    stepped, densities = refs[2 * count + 1 : 3 * count + 1], refs[3 * count + 1 :]
    for state, change, out in zip(states, changes, stepped):
        out[...] = state[...] - time_step * change[...]
    for t, out in enumerate(densities):
        width, modes = out.shape[:2]
        for mode in range(modes):
            at = (t * 8 + mode) * 8
            out[:, mode, :] = sums[:width, at : at + width] * (1.0 / float(width ** (modes - 1)))


def flow_kernel(plan, chunks, combos, layers, wide, *refs):
    count = len(plan)
    spare = list(refs)

    def take(number):
        taken = spare[:number]
        del spare[:number]
        return taken

    parts = len(chunks)
    sends, states = take(parts), take(count)
    intersections, positions = take(2)
    operators = take(count)
    (coupling,) = take(1)
    kinds = [item["kind"] for item in plan]
    tables = [take(max(kinds) + 1) for _ in range(8)]
    lead_pick, lead_turned, lead_rest, lead_rest_turned, tail_pick, tail_turned, tail_rest, tail_rest_turned = [
        [table[kind] for kind in kinds] for table in tables
    ]
    changes = take(count)
    (sums_out,) = take(1)
    gathered, mixed, back = take(parts), take(parts), take(parts)
    value, result = take(2)
    matrices = [take(len(item["targets"])) for item in plan]
    tails = {key: take(1 if key[0] == key[1] else 2) for key in combos}
    cubes, totals = take(count), take(count)
    zero_in, one_in, zero_out, one_out = take(4)
    inner_over, inner_pos, full_over, full_pos = take(4)
    small, splats, sums, stage, layer_sums, rows_of_sums = take(6)
    across_send, across_recv, up_send, up_recv, down_send, down_recv, home_send, home_recv, own, sum_send, sum_recv = spare

    sub = lax.axis_size("sub")
    me = lax.axis_index("grp") * sub + lax.axis_index("sub")
    layer, place = me // wide, me % wide

    def device(at_layer, at_place):
        index = at_layer * wide + at_place
        return (index // sub, index % sub)

    def peer(step):
        return lax.rem(place + step, wide)

    def across(t, step):
        return pltpu.make_async_remote_copy(
            src_ref=sends[t].at[peer(step)],
            dst_ref=gathered[t].at[layer, place],
            send_sem=across_send.at[t, step],
            recv_sem=across_recv.at[t, step],
            device_id=device(layer, peer(step)),
            device_id_type=mesh_ids,
        )

    def home(t, step):
        return pltpu.make_async_remote_copy(
            src_ref=mixed[t].at[peer(step)],
            dst_ref=back[t].at[place],
            send_sem=home_send.at[t, step],
            recv_sem=home_recv.at[t, step],
            device_id=device(layer, peer(step)),
            device_id_type=mesh_ids,
        )

    def hop(t, step, up):
        block = layer - step if up else layer + step
        return pltpu.make_async_remote_copy(
            src_ref=gathered[t].at[block],
            dst_ref=gathered[t].at[block],
            send_sem=(up_send if up else down_send).at[t, step],
            recv_sem=(up_recv if up else down_recv).at[t, step],
            device_id=device(layer + 1 if up else layer - 1, place),
            device_id_type=mesh_ids,
        )

    def sends_hop(step, up):
        if up:
            return jnp.logical_and(layer - step >= 0, layer + 1 < layers)
        return jnp.logical_and(layer + step < layers, layer >= 1)

    def forward(t, step):
        for up in (True, False):
            @pl.when(sends_hop(step, up))
            def _():
                hop(t, step, up).start()

    def arrive(t, step):
        @pl.when(layer - 1 - step >= 0)
        def _():
            pltpu.make_async_remote_copy(
                src_ref=gathered[t].at[layer - 1 - step],
                dst_ref=gathered[t].at[layer - 1 - step],
                send_sem=up_send.at[t, step],
                recv_sem=up_recv.at[t, step],
                device_id=device(layer - 1, place),
                device_id_type=mesh_ids,
            ).wait_recv()

        @pl.when(layer + 1 + step < layers)
        def _():
            pltpu.make_async_remote_copy(
                src_ref=gathered[t].at[layer + 1 + step],
                dst_ref=gathered[t].at[layer + 1 + step],
                send_sem=down_send.at[t, step],
                recv_sem=down_recv.at[t, step],
                device_id=device(layer + 1, place),
                device_id_type=mesh_ids,
            ).wait_recv()

    def keep(t):
        return pltpu.make_async_copy(sends[t].at[place], gathered[t].at[layer, place], own.at[t])

    def keep_home(t):
        return pltpu.make_async_copy(mixed[t].at[place], back[t].at[place], own.at[parts + t])

    def layer_ready(t):
        keep(t).wait()
        for step in range(1, wide):
            across(t, step).wait_recv()

    def put_density(more, t, mode, block):
        at = (t * 8 + mode) * 8
        sums[:, at : at + 8] = sums[:, at : at + 8] + block if more else block

    def add_density(more, t, mode, gram, rest_rows, rest_columns, pick, turned):
        kept = split(jnp.where(rest_rows == rest_columns, gram, 0.0))
        chosen = pick.astype(jnp.bfloat16)
        dims = (((1,), (1,)), ((), ()))
        right = lax.dot_general(kept[0], chosen, dims, preferred_element_type=jnp.float32) + lax.dot_general(
            kept[1], chosen, dims, preferred_element_type=jnp.float32
        )
        block = lax.dot_general(
            turned, right, (((0,), (0,)), ((), ())), precision=highest, preferred_element_type=jnp.float32
        )
        put_density(more, t, mode, 0.5 * (block + block.T))

    def mix(c):
        t, first, tiles = chunks[c]
        item = plan[t]
        rows, slot = item["rows"], item["slot"]
        depth = layers * wide * slot
        value[:depth, : tiles * lanes] = jnp.zeros((depth, tiles * lanes), jnp.float32)

        @pl.loop(0, layers)
        def _(at_layer):
            @pl.loop(0, wide)
            def _(at_place):
                base = pl.multiple_of((at_layer * wide + at_place) * slot, slot)
                for tile in range(tiles):
                    value[pl.ds(base, rows), tile * lanes : (tile + 1) * lanes] = gathered[c][
                        at_layer, at_place, tile * rows : (tile + 1) * rows, :
                    ]

        blocks = []
        for matrix in matrices[t]:
            blocks.append(split(matrix[...]))
        mine = pl.ds(pl.multiple_of(layer * wide * slot, 8), wide * slot)
        gram = None
        for start in range(0, tiles, 2):
            wide_tiles = min(2, tiles - start)
            span = slice(start * lanes, (start + wide_tiles) * lanes)
            data = split(value[:depth, span])
            own_rows = split(value[mine, span])
            part = lax.dot_general(
                own_rows[0], data[0], (((1,), (1,)), ((), ())), preferred_element_type=jnp.float32
            ) + 2.0 * lax.dot_general(
                own_rows[0], data[1], (((1,), (1,)), ((), ())), preferred_element_type=jnp.float32
            )
            gram = part if gram is None else gram + part
            offset = 0
            for block, target in zip(blocks, item["targets"]):
                size = target * wide
                result[:size, : wide_tiles * lanes] = dot3(block, data, ((1,), (0,)))
                for at_place in range(wide):
                    for tile in range(wide_tiles):
                        row = offset + (start + tile) * target
                        mixed[c][at_place, row : row + target, :] = result[
                            at_place * target : (at_place + 1) * target, tile * lanes : (tile + 1) * lanes
                        ]
                offset += target * tiles
        if mixed[c].shape[1] > offset:
            mixed[c][:, offset:, :] = jnp.zeros((wide, mixed[c].shape[1] - offset, lanes), jnp.float32)
        for k in range(3):
            turned = lead_turned[t][k, mine, :]
            add_density(first > 0, t, k, gram, lead_rest_turned[t][mine, k : k + 1], lead_rest[t][k : k + 1, :], lead_pick[t][k], turned)

    def send_home(t):
        keep_home(t).start()
        for step in range(1, wide):
            home(t, step).start()

    def expand(key, kind, mode, pick):
        matrix = small[(combos[key] * 2 + kind) * 8 + mode]
        out = None
        for b in range(plan[key[1]]["width"]):
            term = matrix[:, b : b + 1] * pick[b : b + 1, :]
            out = term if out is None else out + term
        return out

    def build(key, picks, mode, over_out, pos_out, rows):
        width = plan[key[0]]["width"]
        cols = picks.shape[-1]
        over = [expand(key, 0, mode + k, picks[k]) for k in range(3)]
        pos = [expand(key, 1, mode + k, picks[k]) for k in range(3)]
        square = width * width
        if rows > square * width:
            for out in (over_out, pos_out):
                if out is not None:
                    out[square * width : rows, :cols] = jnp.zeros((rows - square * width, cols), jnp.float32)
        for a in range(width):
            span = slice(a * width, (a + 1) * width)
            inner_over[span, :cols] = over[1][a : a + 1] * over[2][:width]
            inner_pos[span, :cols] = pos[1][a : a + 1] * over[2][:width] + over[1][a : a + 1] * pos[2][:width]
        over_value = inner_over[:square, :cols]
        pos_value = inner_pos[:square, :cols]
        for a in range(width):
            span = slice(a * square, (a + 1) * square)
            pos_out[span, :cols] = pos[0][a : a + 1] * over_value + over[0][a : a + 1] * pos_value
            if over_out is not None:
                over_out[span, :cols] = over[0][a : a + 1] * over_value

    def build_leads(t):
        cols = plan[t]["slot"] * layers * wide
        sources = [t] + [s for s in (t - 1, t + 1) if 0 <= s < count]
        at = 0
        for s in sources:
            rows = plan[s]["rows"]
            build((s, t), lead_pick[t], 0, full_over if s != t else None, full_pos, rows * layers * wide)
            mine = pl.ds(pl.multiple_of(layer * rows * wide, 8), rows * wide)
            for full in (full_over, full_pos) if s != t else (full_pos,):
                matrices[t][at][...] = full[mine, :cols]
                at += 1

    def build_tail(s, t):
        outs = tails[(s, t)]
        build((t, s), tail_pick[s], 5, outs[0] if s != t else None, outs[-1], plan[t]["width"] ** 3)

    def cube(s):
        item = plan[s]
        rows, slot, width = item["rows"], item["slot"], item["width"]
        size = width**3
        cubes[s][...] = jnp.zeros(cubes[s].shape, jnp.float32)
        for q in range(width**2):
            cubes[s][q * slot : q * slot + rows, :size] = states[s][:, q * size : (q + 1) * size]

    def scalar(key, kind, mode, a, b):
        row = ((combos[key] * 2 + kind) * 2 + mode) * 64 + b * 8 + a
        return splats[row : row + 1, :]

    def prepare():
        small[...] = jnp.zeros(small.shape, jnp.float32)
        pair, mode_of, strength = coupling[0:1, :], coupling[1:2, :], coupling[2:3, :]
        for p in range(count - 1):
            rows, cols = plan[p]["width"], plan[p + 1]["width"]
            for k in range(8):
                chosen = jnp.logical_and(pair == float(p), mode_of == float(k))
                weight = jnp.sum(jnp.where(chosen, strength, 0.0), axis=1, keepdims=True)
                for kind, source in enumerate((intersections, positions)):
                    block = source[p, :rows, k, :cols]
                    if kind:
                        block = weight * block
                    at = (combos[(p, p + 1)] * 2 + kind) * 8 + k
                    small[at, :rows, :cols] = block
                    small[(combos[(p + 1, p)] * 2 + kind) * 8 + k] = small[at].T
        row = lax.broadcasted_iota(jnp.int32, (8, 8), 0)
        column = lax.broadcasted_iota(jnp.int32, (8, 8), 1)
        for t in range(count):
            width = plan[t]["width"]
            unit = jnp.where(jnp.logical_and(row == column, row < width), 1.0, 0.0)
            for k in range(8):
                small[combos[(t, t)] * 16 + k] = unit
                at = combos[(t, t)] * 16 + 8 + k
                small[at, :width, :width] = operators[t][:, k, :]
                if k >= 5:
                    small[at] = small[at].T
        for key in combos:
            for kind in range(2):
                for mode in range(2):
                    matrix = small[(combos[key] * 2 + kind) * 8 + 3 + mode]
                    base = ((combos[key] * 2 + kind) * 2 + mode) * 64
                    for b in range(8):
                        splats[base + b * 8 : base + b * 8 + 8, :] = jnp.broadcast_to(matrix[:, b : b + 1], (8, lanes))

    def self_part(s):
        item = plan[s]
        slot, width = item["slot"], item["width"]
        size = width**3
        total = totals[s]
        total[:, :size] = dot3(split(cubes[s][:, :size]), split(tails[(s, s)][0][:, :size]), ((1,), (0,)))
        block = width * slot
        for tile in range(-(-size // lanes)):
            at = slice(tile * lanes, (tile + 1) * lanes)

            @pl.loop(0, width)
            def _(i):
                base = pl.multiple_of(i * block, 8)
                held = [cubes[s][pl.ds(base + b * slot, slot), at] for b in range(width)]
                for a in range(width):
                    out = total[pl.ds(base + a * slot, slot), at]
                    for b in range(width):
                        out = out + scalar((s, s), 1, 1, a, b) * held[b]
                    total[pl.ds(base + a * slot, slot), at] = out

            @pl.loop(0, width)
            def _(i):
                base = pl.multiple_of(i * slot, 8)
                held = [cubes[s][pl.ds(base + b * block, slot), at] for b in range(width)]
                for a in range(width):
                    out = total[pl.ds(base + a * block, slot), at]
                    for b in range(width):
                        out = out + scalar((s, s), 1, 0, a, b) * held[b]
                    total[pl.ds(base + a * block, slot), at] = out

    def self_density(s):
        item = plan[s]
        slot, width = item["slot"], item["width"]
        size = width**3
        data = split(cubes[s][:, :size])
        gram = None
        step = width * slot
        dims = (((0,), (0,)), ((), ()))
        gram = lax.dot_general(data[0], data[0], dims, preferred_element_type=jnp.float32) + 2.0 * lax.dot_general(
            data[0], data[1], dims, preferred_element_type=jnp.float32
        )
        for k in range(3):
            add_density(
                False, s, 5 + k, gram, tail_rest_turned[s][:, k : k + 1], tail_rest[s][k : k + 1, :], tail_pick[s][k], tail_turned[s][k]
            )
        column = lax.broadcasted_iota(jnp.int32, (8, 8), 1)
        wide_lanes = cubes[s].shape[1]
        rows_of_sums[...] = jnp.zeros(rows_of_sums.shape, jnp.float32)
        for mode in range(2):
            block = jnp.zeros((8, 8), jnp.float32)
            for i in range(width):
                for j in range(width):
                    row = None
                    for other in range(width):
                        left = (i * width + other if mode == 0 else other * width + i) * slot
                        right = (j * width + other if mode == 0 else other * width + j) * slot
                        term = cubes[s][left : left + slot, :] * cubes[s][right : right + slot, :]
                        row = term if row is None else row + term
                    rows_of_sums[j : j + 1, :wide_lanes] = jnp.sum(row, axis=0, keepdims=True)
                column_sum = jnp.sum(rows_of_sums[:, :wide_lanes], axis=1, keepdims=True)
                block = jnp.where(column == i, column_sum, block)
            put_density(False, s, 3 + mode, block)

    def pieces(c):
        t, first, tiles = chunks[c]
        columns, size = plan[t]["columns"], plan[t]["width"] ** 3
        out = []
        for at_place in range(wide):
            for tile in range(tiles):
                start = (at_place * plan[t]["tiles"] + first + tile) * lanes
                stop = min(start + lanes, columns)
                while start < stop:
                    q = start // size
                    end = min(stop, (q + 1) * size)
                    out.append((at_place, tile, start % lanes, end - start, q, start - q * size))
                    start = end
        return out

    def wait_home(c):
        keep_home(c).wait()
        for step in range(1, wide):
            home(c, step).wait_recv()

    def flat(s):
        item = plan[s]
        rows, slot, size = item["rows"], item["slot"], item["width"] ** 3
        for q in range(item["width"] ** 2):
            changes[s][:, q * size : (q + 1) * size] = totals[s][q * slot : q * slot + rows, :size]

    def add_action(c):
        t, first, tiles = chunks[c]
        item = plan[t]
        rows = item["rows"]
        for at_place in range(wide):
            for tile in range(tiles):
                start = (at_place * item["tiles"] + first + tile) * lanes
                width = min(lanes, item["columns"] - start)
                if width > 0:
                    changes[t][:, start : start + width] += back[c][at_place, tile * rows : (tile + 1) * rows, :width]

    def pair_part(s, t):
        item = plan[t]
        rows, slot = plan[s]["rows"], plan[s]["slot"]
        wide_in, wide_out, size = item["width"], plan[s]["width"], item["width"] ** 3
        before = item["rows"]
        if s > t and t > 0:
            before += 2 * plan[t - 1]["rows"]
        for c, chunk in enumerate(chunks):
            if chunk[0] != t:
                continue
            offset = before * chunk[2]
            for target in (zero_in, one_in):
                for at_place, tile, lane, length, q, inside in pieces(c):
                    row = offset + tile * rows
                    target[q * slot : q * slot + rows, inside : inside + length] = back[c][
                        at_place, row : row + rows, lane : lane + length
                    ]
                offset += rows * chunk[2]

        def stage_of(mode, loops, step, in_stride, out_stride, out_step, zero_from, one_from, zero_to, one_to):
            for tile in range(-(-size // lanes)):
                at = slice(tile * lanes, (tile + 1) * lanes)

                @pl.loop(0, loops)
                def _(i):
                    base = pl.multiple_of(i * step, 8)
                    out_base = pl.multiple_of(i * out_step, 8)
                    for group in range(0, slot, 8):
                        zero = [zero_from[pl.ds(base + b * in_stride + group, 8), at] for b in range(wide_in)]
                        one = [one_from[pl.ds(base + b * in_stride + group, 8), at] for b in range(wide_in)]
                        for a in range(wide_out):
                            next_zero, next_one = None, None
                            for b in range(wide_in):
                                over, pos = scalar((s, t), 0, mode, a, b), scalar((s, t), 1, mode, a, b)
                                zero_term, one_term = over * zero[b], over * one[b] + pos * zero[b]
                                next_zero = zero_term if b == 0 else next_zero + zero_term
                                next_one = one_term if b == 0 else next_one + one_term
                            zero_to[pl.ds(out_base + a * out_stride + group, 8), at] = next_zero
                            one_to[pl.ds(out_base + a * out_stride + group, 8), at] = next_one

        stage_of(1, wide_in, wide_in * slot, slot, slot, wide_out * slot, zero_in, one_in, zero_out, one_out)
        stage_of(0, wide_out, slot, wide_out * slot, wide_out * slot, slot, zero_out, one_out, zero_in, one_in)
        live = wide_out**2 * slot
        out_size = wide_out**3
        over_tail, pos_tail = tails[(s, t)]
        totals[s][:, :out_size] += dot3(
            split(one_in[:live, :size]), split(over_tail[:, :out_size]), ((1,), (0,))
        ) + dot3(split(zero_in[:live, :size]), split(pos_tail[:, :out_size]), ((1,), (0,)))

    def first_sum(step):
        return pltpu.make_async_remote_copy(
            src_ref=sums,
            dst_ref=stage.at[place],
            send_sem=sum_send.at[step],
            recv_sem=sum_recv.at[step],
            device_id=device(layer, peer(step)),
            device_id_type=mesh_ids,
        )

    def second_sum(step):
        return pltpu.make_async_remote_copy(
            src_ref=layer_sums.at[layer],
            dst_ref=layer_sums.at[layer],
            send_sem=sum_send.at[wide + step],
            recv_sem=sum_recv.at[wide + step],
            device_id=device(lax.rem(layer + step, layers), place),
            device_id_type=mesh_ids,
        )

    barrier = pltpu.get_barrier_semaphore()
    for step in range(1, wide):
        pl.semaphore_signal(barrier, inc=1, device_id=device(layer, peer(step)), device_id_type=mesh_ids)
    for step in range(1, layers):
        pl.semaphore_signal(
            barrier, inc=1, device_id=device(lax.rem(layer + step, layers), place), device_id_type=mesh_ids
        )
    pl.semaphore_wait(barrier, wide + layers - 2)

    hops = layers - 1
    of = [[c for c in range(parts) if chunks[c][0] == t] for t in range(count)]
    early, late = of[1], of[0]
    rest = [c for t in range(2, count) for c in of[t]]
    for c in early + late + rest:
        keep(c).start()
        for step in range(1, wide):
            across(c, step).start()

    def begin(c):
        layer_ready(c)
        forward(c, 0)

    def relay(c, step):
        if step < hops:
            arrive(c, step - 1)
            forward(c, step)

    def relays(some, steps):
        for step in steps:
            for c in some:
                relay(c, step)

    def gathered_now(some):
        if hops:
            for c in some:
                arrive(c, hops - 1)

    prepare()
    for c in early:
        begin(c)
    build_leads(1)
    for c in late[:1]:
        begin(c)
    relays(early, (1,))
    for c in late[1:]:
        begin(c)
    for t in range(count):
        if t != 1:
            build_leads(t)
    relays(late[:1], (1,))
    relays(early, (2,))
    for s in range(count):
        cube(s)
    relays(late[1:], (1,))
    relays(early, range(3, hops))
    for s in range(count):
        build_tail(s, s)
    self_part(0)
    relays(late[:1], (2,))
    gathered_now(early)
    for c in early:
        mix(c)
    relays(late[1:], (2,))
    for c in early:
        send_home(c)
    for c in rest:
        begin(c)
    relays(late, range(3, hops))
    for s in range(count):
        for t in (s - 1, s + 1):
            if 0 <= t < count:
                build_tail(s, t)
    self_density(0)
    for c in late:
        gathered_now([c])
        mix(c)
        relays(rest, (1,) if c == late[0] else ())
        send_home(c)
    for s in range(1, count):
        self_part(s)
    relays(rest, range(2, hops))
    for c in early:
        wait_home(c)
    pair_part(0, 1)
    for s in range(1, count):
        self_density(s)
    gathered_now(rest)
    for c in rest:
        mix(c)
    for step in range(1, wide):
        first_sum(step).start()
    stage[place] = sums[...]
    for c in rest:
        send_home(c)
    pair_part(2, 1)
    flat(0)
    for c in late:
        wait_home(c)
    for c in late:
        add_action(c)
    pair_part(1, 0)
    for step in range(1, wide):
        first_sum(step).wait()
    layer_sums[layer] = jnp.sum(stage[...], axis=0)
    for t in range(2, count):
        for c in of[t]:
            wait_home(c)
        for s in (t - 1, t + 1):
            if 0 <= s < count:
                pair_part(s, t)
        if t == 2:
            for step in range(1, layers):
                second_sum(step).start()
        flat(t - 1)
        for c in of[t - 1]:
            add_action(c)
    flat(count - 1)
    for c in of[count - 1]:
        add_action(c)
    for step in range(1, layers):
        second_sum(step).wait()
    sums_out[...] = jnp.sum(layer_sums[...], axis=0)

    for c in range(parts):
        for step in range(1, wide):
            across(c, step).wait_send()
            home(c, step).wait_send()
        for step in range(hops):
            for up in (True, False):
                @pl.when(sends_hop(step, up))
                def _():
                    hop(c, step, up).wait_send()


def call(kernel, outs, scratch, *args, name, remote=None):
    extra = params
    if remote is not None:
        extra = pltpu.CompilerParams(vmem_limit_bytes=vmem_limit, collective_id=remote, has_side_effects=True)
    return pl.pallas_call(
        kernel,
        out_shape=[jax.ShapeDtypeStruct(shape, jnp.float32) for shape in outs],
        in_specs=[vmem] * len(args),
        out_specs=[vmem] * len(outs),
        scratch_shapes=[pltpu.VMEM(shape, jnp.float32) if isinstance(shape, tuple) else shape for shape in scratch],
        compiler_params=extra,
        name=name,
    )(*args)


def round_up(value, unit):
    return -(-value // unit) * unit


def spread(table, rows, slot):
    shape = table.shape[:-1]
    held = table.reshape(shape + (-1, rows))
    wider = np.full(shape + (held.shape[-2], slot), -1 if table.dtype == np.int32 else 0, table.dtype)
    wider[..., :rows] = held
    return wider.reshape(shape + (-1,))


def local(*args):
    states = args[:4]
    operators = args[4:8]
    intersections, positions, coupling_pair, coupling_mode, coupling_strength = args[8:]
    devices = lax.axis_size("grp") * lax.axis_size("sub")
    count = len(states)
    widths = [operator.shape[1] for operator in operators]
    rows = [state.shape[0] for state in states]
    columns = [state.shape[1] for state in states]
    totals = [size * devices for size in rows]
    layers = max(1, lax.axis_size("grp") // 4)
    wide = devices // layers
    tiles = [-(-size // (wide * lanes)) for size in columns]
    slots = [round_up(size, 8) for size in rows]
    pairs, modes = intersections.shape[:2]

    combos = {}
    for p in range(pairs):
        combos[(p, p + 1)] = len(combos)
        combos[(p + 1, p)] = len(combos)
    for s in range(count):
        combos[(s, s)] = len(combos)

    order = [[(t, "pos")] + [(s, kind) for s in (t - 1, t + 1) if 0 <= s < count for kind in ("over", "pos")] for t in range(count)]
    kinds = list(dict.fromkeys(zip(widths, rows)))
    plan = [
        dict(
            rows=rows[t],
            slot=slots[t],
            tiles=tiles[t],
            columns=columns[t],
            width=widths[t],
            kind=kinds.index((widths[t], rows[t])),
            targets=[rows[s] for s, kind in order[t]],
        )
        for t in range(count)
    ]
    chunks = []
    for t in range(count):
        cut = -(-tiles[t] // 2) if t == 0 else tiles[t]
        for first in range(0, tiles[t], cut):
            chunks.append((t, first, min(cut, tiles[t] - first)))
    sends = call(
        functools.partial(pack_kernel, plan, chunks),
        [(wide, round_up(rows[t] * number, 8), lanes) for t, first, number in chunks],
        [],
        *states,
        name="pack",
    )
    back_shapes = [(wide, round_up(sum(plan[t]["targets"]) * number, 8), lanes) for t, first, number in chunks]
    coupling = jnp.stack(
        [coupling_pair.astype(jnp.float32), coupling_mode.astype(jnp.float32), coupling_strength]
    )
    tables = {name: [] for name in ("pick", "turned", "rest", "rest_turned")}
    for lead in (True, False):
        for width, held in kinds:
            size = held * devices if lead else width**3
            pick = np.zeros((3, 8, size), np.float32)
            rest = np.stack([others(width, 3, size, place) for place in range(3)])
            for place in range(3):
                pick[place, :width] = digits(width, 3, size, place)
            if lead:
                rest, pick = spread(rest, held, round_up(held, 8)), spread(pick, held, round_up(held, 8))
            tables["pick"].append(jnp.asarray(pick))
            tables["turned"].append(jnp.asarray(np.ascontiguousarray(pick.transpose(0, 2, 1))))
            tables["rest"].append(jnp.asarray(rest))
            tables["rest_turned"].append(jnp.asarray(np.ascontiguousarray(rest.T)))
    names = ("pick", "turned", "rest", "rest_turned")
    constants = [item for name in names for item in tables[name][: len(kinds)]] + [
        item for name in names for item in tables[name][len(kinds) :]
    ]
    cube_shapes = [(widths[s] ** 2 * slots[s], round_up(widths[s] ** 3, lanes)) for s in range(count)]
    mixed_shape = (max(widths) ** 2 * max(slots), round_up(max(widths) ** 3, lanes))
    depths = [devices * slots[t] for t in range(count)]
    dma = pltpu.SemaphoreType.DMA
    sum_shape = (8, count * 64)
    flowed = call(
        functools.partial(flow_kernel, plan, chunks, combos, layers, wide),
        [state.shape for state in states] + [sum_shape],
        [(layers,) + send.shape for send in sends]
        + back_shapes * 2
        + [(max(depths), max(number for t, first, number in chunks) * lanes), (wide * max(rows), 2 * lanes)]
        + [(wide * rows[s], depths[t]) for t in range(count) for s, kind in order[t]]
        + [(widths[t] ** 3, round_up(widths[s] ** 3, lanes)) for s, t in combos for _ in range(1 if s == t else 2)]
        + cube_shapes * 2
        + [mixed_shape] * 4
        + [(round_up(max(widths) ** 2, 8), max(depths + [mixed_shape[1]]))] * 2
        + [(max(totals), max(depths))] * 2
        + [(len(combos) * 16, 8, 8), (len(combos) * 256, lanes)]
        + [sum_shape, (wide,) + sum_shape, (layers,) + sum_shape, (8, mixed_shape[1])]
        + [dma((len(chunks), wide))] * 2
        + [dma((len(chunks), layers))] * 4
        + [dma((len(chunks), wide))] * 2
        + [dma((2 * len(chunks),))]
        + [dma((wide + layers,))] * 2,
        *sends,
        *states,
        jnp.transpose(intersections, (0, 2, 1, 3)),
        jnp.transpose(positions, (0, 2, 1, 3)),
        *[jnp.transpose(operator, (1, 0, 2)) for operator in operators],
        coupling,
        *constants,
        name="flow",
        remote=0,
    )
    finished = call(
        functools.partial(finish_kernel, count),
        [state.shape for state in states] + [(widths[t], modes, widths[t]) for t in range(count)],
        [],
        *states,
        *flowed,
        name="finish",
    )
    return tuple(finished[:count]) + tuple(jnp.transpose(item, (1, 0, 2)) for item in finished[count:])


def solution(mesh):
    sharded = P(("grp", "sub"), None)
    return jax.shard_map(
        local,
        mesh=mesh,
        in_specs=(sharded,) * 4 + (P(),) * 9,
        out_specs=(sharded,) * 4 + (P(),) * 4,
        check_vma=False,
    )
```

```python
import functools
import math

import jax
import jax.numpy as jnp
import numpy as np
from jax import lax
from jax.experimental import pallas as pl
from jax.experimental.pallas import tpu as pltpu
from jax.sharding import PartitionSpec as P

highest = lax.Precision.HIGHEST
time_step = 0.25
lanes = 128
vmem_limit = 63 * 1024 * 1024
params = pltpu.CompilerParams(vmem_limit_bytes=vmem_limit)
vmem = pl.BlockSpec(memory_space=pltpu.VMEM)
mesh_ids = pl.DeviceIdType.MESH


def digits(width, count, total, place):
    index = np.arange(total)
    live = index < width**count
    digit = (index // width ** (count - 1 - place)) % width
    return ((digit[None, :] == np.arange(width)[:, None]) & live[None, :]).astype(np.float32)


def others(width, count, total, place):
    index = np.arange(total)
    stride = width ** (count - 1 - place)
    rest = index - ((index // stride) % width) * stride
    return np.where(index < width**count, rest, -1).astype(np.int32)


def split(value):
    top = value.astype(jnp.bfloat16)
    return top, (value - top.astype(jnp.float32)).astype(jnp.bfloat16)


def dot3(left, right, contract):
    dims = (contract, ((), ()))
    go = functools.partial(lax.dot_general, dimension_numbers=dims, preferred_element_type=jnp.float32)
    return go(left[0], right[0]) + (go(left[0], right[1]) + go(left[1], right[0]))


def pack_kernel(plan, chunks, *refs):
    count = len(plan)
    sources = refs[:count]
    for out, (t, first, number) in zip(refs[count:], chunks):
        source, item = sources[t], plan[t]
        rows = item["rows"]
        used = number * rows
        if out.shape[1] > used:
            out[:, used:, :] = jnp.zeros((out.shape[0], out.shape[1] - used, lanes), jnp.float32)
        for device in range(out.shape[0]):
            for tile in range(number):
                start = (device * item["tiles"] + first + tile) * lanes
                width = min(lanes, item["columns"] - start)
                at = slice(tile * rows, (tile + 1) * rows)
                if width < lanes:
                    out[device, at, :] = jnp.zeros((rows, lanes), jnp.float32)
                if width > 0:
                    out[device, at, :width] = source[:, start : start + width]


def finish_kernel(count, *refs):
    states, changes, sums = refs[:count], refs[count : 2 * count], refs[2 * count]
    stepped, densities = refs[2 * count + 1 : 3 * count + 1], refs[3 * count + 1 :]
    for state, change, out in zip(states, changes, stepped):
        out[...] = state[...] - time_step * change[...]
    for t, out in enumerate(densities):
        width, modes = out.shape[:2]
        for mode in range(modes):
            at = (t * 8 + mode) * 8
            out[:, mode, :] = sums[:width, at : at + width] * (1.0 / float(width ** (modes - 1)))


def flow_kernel(plan, chunks, combos, layers, wide, *refs):
    count = len(plan)
    spare = list(refs)

    def take(number):
        taken = spare[:number]
        del spare[:number]
        return taken

    parts = len(chunks)
    sends, states = take(parts), take(count)
    intersections, positions = take(2)
    operators = take(count)
    (coupling,) = take(1)
    kinds = [item["kind"] for item in plan]
    tables = [take(max(kinds) + 1) for _ in range(8)]
    lead_pick, lead_turned, lead_rest, lead_rest_turned, tail_pick, tail_turned, tail_rest, tail_rest_turned = [
        [table[kind] for kind in kinds] for table in tables
    ]
    changes = take(count)
    (sums_out,) = take(1)
    gathered, mixed, back = take(parts), take(parts), take(parts)
    value, result = take(2)
    matrices = [take(len(item["targets"])) for item in plan]
    tails = {key: take(1 if key[0] == key[1] else 2) for key in combos}
    cubes, totals = take(count), take(count)
    zero_in, one_in, zero_out, one_out = take(4)
    inner_over, inner_pos, full_over, full_pos = take(4)
    small, splats, sums, stage, layer_sums, rows_of_sums = take(6)
    across_send, across_recv, up_send, up_recv, down_send, down_recv, home_send, home_recv, own, sum_send, sum_recv = spare

    sub = lax.axis_size("sub")
    me = lax.axis_index("grp") * sub + lax.axis_index("sub")
    layer, place = me // wide, me % wide

    def device(at_layer, at_place):
        index = at_layer * wide + at_place
        return (index // sub, index % sub)

    def peer(step):
        return lax.rem(place + step, wide)

    def across(t, step):
        return pltpu.make_async_remote_copy(
            src_ref=sends[t].at[peer(step)],
            dst_ref=gathered[t].at[layer, place],
            send_sem=across_send.at[t, step],
            recv_sem=across_recv.at[t, step],
            device_id=device(layer, peer(step)),
            device_id_type=mesh_ids,
        )

    def home(t, step):
        return pltpu.make_async_remote_copy(
            src_ref=mixed[t].at[peer(step)],
            dst_ref=back[t].at[place],
            send_sem=home_send.at[t, step],
            recv_sem=home_recv.at[t, step],
            device_id=device(layer, peer(step)),
            device_id_type=mesh_ids,
        )

    def hop(t, step, up):
        block = layer - step if up else layer + step
        return pltpu.make_async_remote_copy(
            src_ref=gathered[t].at[block],
            dst_ref=gathered[t].at[block],
            send_sem=(up_send if up else down_send).at[t, step],
            recv_sem=(up_recv if up else down_recv).at[t, step],
            device_id=device(layer + 1 if up else layer - 1, place),
            device_id_type=mesh_ids,
        )

    def sends_hop(step, up):
        if up:
            return jnp.logical_and(layer - step >= 0, layer + 1 < layers)
        return jnp.logical_and(layer + step < layers, layer >= 1)

    def forward(t, step):
        for up in (True, False):
            @pl.when(sends_hop(step, up))
            def _():
                hop(t, step, up).start()

    def arrive(t, step):
        @pl.when(layer - 1 - step >= 0)
        def _():
            pltpu.make_async_remote_copy(
                src_ref=gathered[t].at[layer - 1 - step],
                dst_ref=gathered[t].at[layer - 1 - step],
                send_sem=up_send.at[t, step],
                recv_sem=up_recv.at[t, step],
                device_id=device(layer - 1, place),
                device_id_type=mesh_ids,
            ).wait_recv()

        @pl.when(layer + 1 + step < layers)
        def _():
            pltpu.make_async_remote_copy(
                src_ref=gathered[t].at[layer + 1 + step],
                dst_ref=gathered[t].at[layer + 1 + step],
                send_sem=down_send.at[t, step],
                recv_sem=down_recv.at[t, step],
                device_id=device(layer + 1, place),
                device_id_type=mesh_ids,
            ).wait_recv()

    def keep(t):
        return pltpu.make_async_copy(sends[t].at[place], gathered[t].at[layer, place], own.at[t])

    def keep_home(t):
        return pltpu.make_async_copy(mixed[t].at[place], back[t].at[place], own.at[parts + t])

    def layer_ready(t):
        keep(t).wait()
        for step in range(1, wide):
            across(t, step).wait_recv()

    def put_density(more, t, mode, block):
        at = (t * 8 + mode) * 8
        sums[:, at : at + 8] = sums[:, at : at + 8] + block if more else block

    def add_density(more, t, mode, gram, rest_rows, rest_columns, pick, turned):
        kept = split(jnp.where(rest_rows == rest_columns, gram, 0.0))
        chosen = pick.astype(jnp.bfloat16)
        dims = (((1,), (1,)), ((), ()))
        right = lax.dot_general(kept[0], chosen, dims, preferred_element_type=jnp.float32) + lax.dot_general(
            kept[1], chosen, dims, preferred_element_type=jnp.float32
        )
        block = lax.dot_general(
            turned, right, (((0,), (0,)), ((), ())), precision=highest, preferred_element_type=jnp.float32
        )
        put_density(more, t, mode, 0.5 * (block + block.T))

    def mix(c):
        t, first, tiles = chunks[c]
        item = plan[t]
        rows, slot = item["rows"], item["slot"]
        depth = layers * wide * slot
        value[:depth, : tiles * lanes] = jnp.zeros((depth, tiles * lanes), jnp.float32)

        @pl.loop(0, layers)
        def _(at_layer):
            @pl.loop(0, wide)
            def _(at_place):
                base = pl.multiple_of((at_layer * wide + at_place) * slot, slot)
                for tile in range(tiles):
                    value[pl.ds(base, rows), tile * lanes : (tile + 1) * lanes] = gathered[c][
                        at_layer, at_place, tile * rows : (tile + 1) * rows, :
                    ]

        blocks = []
        for matrix in matrices[t]:
            blocks.append(split(matrix[...]))
        mine = pl.ds(pl.multiple_of(layer * wide * slot, 8), wide * slot)
        gram = None
        for start in range(0, tiles, 2):
            wide_tiles = min(2, tiles - start)
            span = slice(start * lanes, (start + wide_tiles) * lanes)
            data = split(value[:depth, span])
            own_rows = split(value[mine, span])
            part = lax.dot_general(
                own_rows[0], data[0], (((1,), (1,)), ((), ())), preferred_element_type=jnp.float32
            ) + 2.0 * lax.dot_general(
                own_rows[0], data[1], (((1,), (1,)), ((), ())), preferred_element_type=jnp.float32
            )
            gram = part if gram is None else gram + part
            offset = 0
            for block, target in zip(blocks, item["targets"]):
                size = target * wide
                result[:size, : wide_tiles * lanes] = dot3(block, data, ((1,), (0,)))
                for at_place in range(wide):
                    for tile in range(wide_tiles):
                        row = offset + (start + tile) * target
                        mixed[c][at_place, row : row + target, :] = result[
                            at_place * target : (at_place + 1) * target, tile * lanes : (tile + 1) * lanes
                        ]
                offset += target * tiles
        if mixed[c].shape[1] > offset:
            mixed[c][:, offset:, :] = jnp.zeros((wide, mixed[c].shape[1] - offset, lanes), jnp.float32)
        for k in range(3):
            turned = lead_turned[t][k, mine, :]
            add_density(first > 0, t, k, gram, lead_rest_turned[t][mine, k : k + 1], lead_rest[t][k : k + 1, :], lead_pick[t][k], turned)

    def send_home(t):
        keep_home(t).start()
        for step in range(1, wide):
            home(t, step).start()

    def expand(key, kind, mode, pick):
        matrix = small[(combos[key] * 2 + kind) * 8 + mode]
        out = None
        for b in range(plan[key[1]]["width"]):
            term = matrix[:, b : b + 1] * pick[b : b + 1, :]
            out = term if out is None else out + term
        return out

    def build(key, picks, mode, over_out, pos_out, rows):
        width = plan[key[0]]["width"]
        cols = picks.shape[-1]
        over = [expand(key, 0, mode + k, picks[k]) for k in range(3)]
        pos = [expand(key, 1, mode + k, picks[k]) for k in range(3)]
        square = width * width
        if rows > square * width:
            for out in (over_out, pos_out):
                if out is not None:
                    out[square * width : rows, :cols] = jnp.zeros((rows - square * width, cols), jnp.float32)
        for a in range(width):
            span = slice(a * width, (a + 1) * width)
            inner_over[span, :cols] = over[1][a : a + 1] * over[2][:width]
            inner_pos[span, :cols] = pos[1][a : a + 1] * over[2][:width] + over[1][a : a + 1] * pos[2][:width]
        over_value = inner_over[:square, :cols]
        pos_value = inner_pos[:square, :cols]
        for a in range(width):
            span = slice(a * square, (a + 1) * square)
            pos_out[span, :cols] = pos[0][a : a + 1] * over_value + over[0][a : a + 1] * pos_value
            if over_out is not None:
                over_out[span, :cols] = over[0][a : a + 1] * over_value

    def build_leads(t):
        cols = plan[t]["slot"] * layers * wide
        sources = [t] + [s for s in (t - 1, t + 1) if 0 <= s < count]
        at = 0
        for s in sources:
            rows = plan[s]["rows"]
            build((s, t), lead_pick[t], 0, full_over if s != t else None, full_pos, rows * layers * wide)
            mine = pl.ds(pl.multiple_of(layer * rows * wide, 8), rows * wide)
            for full in (full_over, full_pos) if s != t else (full_pos,):
                matrices[t][at][...] = full[mine, :cols]
                at += 1

    def build_tail(s, t):
        outs = tails[(s, t)]
        build((t, s), tail_pick[s], 5, outs[0] if s != t else None, outs[-1], plan[t]["width"] ** 3)

    def cube(s):
        item = plan[s]
        rows, slot, width = item["rows"], item["slot"], item["width"]
        size = width**3
        cubes[s][...] = jnp.zeros(cubes[s].shape, jnp.float32)
        for q in range(width**2):
            cubes[s][q * slot : q * slot + rows, :size] = states[s][:, q * size : (q + 1) * size]

    def scalar(key, kind, mode, a, b):
        row = ((combos[key] * 2 + kind) * 2 + mode) * 64 + b * 8 + a
        return splats[row : row + 1, :]

    def prepare():
        small[...] = jnp.zeros(small.shape, jnp.float32)
        pair, mode_of, strength = coupling[0:1, :], coupling[1:2, :], coupling[2:3, :]
        for p in range(count - 1):
            rows, cols = plan[p]["width"], plan[p + 1]["width"]
            for k in range(8):
                chosen = jnp.logical_and(pair == float(p), mode_of == float(k))
                weight = jnp.sum(jnp.where(chosen, strength, 0.0), axis=1, keepdims=True)
                for kind, source in enumerate((intersections, positions)):
                    block = source[p, :rows, k, :cols]
                    if kind:
                        block = weight * block
                    at = (combos[(p, p + 1)] * 2 + kind) * 8 + k
                    small[at, :rows, :cols] = block
                    small[(combos[(p + 1, p)] * 2 + kind) * 8 + k] = small[at].T
        row = lax.broadcasted_iota(jnp.int32, (8, 8), 0)
        column = lax.broadcasted_iota(jnp.int32, (8, 8), 1)
        for t in range(count):
            width = plan[t]["width"]
            unit = jnp.where(jnp.logical_and(row == column, row < width), 1.0, 0.0)
            for k in range(8):
                small[combos[(t, t)] * 16 + k] = unit
                at = combos[(t, t)] * 16 + 8 + k
                small[at, :width, :width] = operators[t][:, k, :]
                if k >= 5:
                    small[at] = small[at].T
        for key in combos:
            for kind in range(2):
                for mode in range(2):
                    matrix = small[(combos[key] * 2 + kind) * 8 + 3 + mode]
                    base = ((combos[key] * 2 + kind) * 2 + mode) * 64
                    for b in range(8):
                        splats[base + b * 8 : base + b * 8 + 8, :] = jnp.broadcast_to(matrix[:, b : b + 1], (8, lanes))

    def self_part(s):
        item = plan[s]
        slot, width = item["slot"], item["width"]
        size = width**3
        total = totals[s]
        total[:, :size] = dot3(split(cubes[s][:, :size]), split(tails[(s, s)][0][:, :size]), ((1,), (0,)))
        block = width * slot
        for tile in range(-(-size // lanes)):
            at = slice(tile * lanes, (tile + 1) * lanes)

            @pl.loop(0, width)
            def _(i):
                base = pl.multiple_of(i * block, 8)
                held = [cubes[s][pl.ds(base + b * slot, slot), at] for b in range(width)]
                for a in range(width):
                    out = total[pl.ds(base + a * slot, slot), at]
                    for b in range(width):
                        out = out + scalar((s, s), 1, 1, a, b) * held[b]
                    total[pl.ds(base + a * slot, slot), at] = out

            @pl.loop(0, width)
            def _(i):
                base = pl.multiple_of(i * slot, 8)
                held = [cubes[s][pl.ds(base + b * block, slot), at] for b in range(width)]
                for a in range(width):
                    out = total[pl.ds(base + a * block, slot), at]
                    for b in range(width):
                        out = out + scalar((s, s), 1, 0, a, b) * held[b]
                    total[pl.ds(base + a * block, slot), at] = out

    def self_density(s):
        item = plan[s]
        slot, width = item["slot"], item["width"]
        size = width**3
        data = split(cubes[s][:, :size])
        gram = None
        step = width * slot
        dims = (((0,), (0,)), ((), ()))
        gram = lax.dot_general(data[0], data[0], dims, preferred_element_type=jnp.float32) + 2.0 * lax.dot_general(
            data[0], data[1], dims, preferred_element_type=jnp.float32
        )
        for k in range(3):
            add_density(
                False, s, 5 + k, gram, tail_rest_turned[s][:, k : k + 1], tail_rest[s][k : k + 1, :], tail_pick[s][k], tail_turned[s][k]
            )
        column = lax.broadcasted_iota(jnp.int32, (8, 8), 1)
        wide_lanes = cubes[s].shape[1]
        rows_of_sums[...] = jnp.zeros(rows_of_sums.shape, jnp.float32)
        for mode in range(2):
            block = jnp.zeros((8, 8), jnp.float32)
            for i in range(width):
                for j in range(width):
                    row = None
                    for other in range(width):
                        left = (i * width + other if mode == 0 else other * width + i) * slot
                        right = (j * width + other if mode == 0 else other * width + j) * slot
                        term = cubes[s][left : left + slot, :] * cubes[s][right : right + slot, :]
                        row = term if row is None else row + term
                    rows_of_sums[j : j + 1, :wide_lanes] = jnp.sum(row, axis=0, keepdims=True)
                column_sum = jnp.sum(rows_of_sums[:, :wide_lanes], axis=1, keepdims=True)
                block = jnp.where(column == i, column_sum, block)
            put_density(False, s, 3 + mode, block)

    def pieces(c):
        t, first, tiles = chunks[c]
        columns, size = plan[t]["columns"], plan[t]["width"] ** 3
        out = []
        for at_place in range(wide):
            for tile in range(tiles):
                start = (at_place * plan[t]["tiles"] + first + tile) * lanes
                stop = min(start + lanes, columns)
                while start < stop:
                    q = start // size
                    end = min(stop, (q + 1) * size)
                    out.append((at_place, tile, start % lanes, end - start, q, start - q * size))
                    start = end
        return out

    def wait_home(c):
        keep_home(c).wait()
        for step in range(1, wide):
            home(c, step).wait_recv()

    def flat(s):
        item = plan[s]
        rows, slot, size = item["rows"], item["slot"], item["width"] ** 3
        for q in range(item["width"] ** 2):
            changes[s][:, q * size : (q + 1) * size] = totals[s][q * slot : q * slot + rows, :size]

    def add_action(c):
        t, first, tiles = chunks[c]
        item = plan[t]
        rows = item["rows"]
        for at_place in range(wide):
            for tile in range(tiles):
                start = (at_place * item["tiles"] + first + tile) * lanes
                width = min(lanes, item["columns"] - start)
                if width > 0:
                    changes[t][:, start : start + width] += back[c][at_place, tile * rows : (tile + 1) * rows, :width]

    def pair_part(s, t):
        item = plan[t]
        rows, slot = plan[s]["rows"], plan[s]["slot"]
        wide_in, wide_out, size = item["width"], plan[s]["width"], item["width"] ** 3
        before = item["rows"]
        if s > t and t > 0:
            before += 2 * plan[t - 1]["rows"]
        for c, chunk in enumerate(chunks):
            if chunk[0] != t:
                continue
            offset = before * chunk[2]
            for target in (zero_in, one_in):
                for at_place, tile, lane, length, q, inside in pieces(c):
                    row = offset + tile * rows
                    target[q * slot : q * slot + rows, inside : inside + length] = back[c][
                        at_place, row : row + rows, lane : lane + length
                    ]
                offset += rows * chunk[2]

        def stage_of(mode, loops, step, in_stride, out_stride, out_step, zero_from, one_from, zero_to, one_to):
            for tile in range(-(-size // lanes)):
                at = slice(tile * lanes, (tile + 1) * lanes)

                @pl.loop(0, loops)
                def _(i):
                    base = pl.multiple_of(i * step, 8)
                    out_base = pl.multiple_of(i * out_step, 8)
                    for group in range(0, slot, 8):
                        zero = [zero_from[pl.ds(base + b * in_stride + group, 8), at] for b in range(wide_in)]
                        one = [one_from[pl.ds(base + b * in_stride + group, 8), at] for b in range(wide_in)]
                        for a in range(wide_out):
                            next_zero, next_one = None, None
                            for b in range(wide_in):
                                over, pos = scalar((s, t), 0, mode, a, b), scalar((s, t), 1, mode, a, b)
                                zero_term, one_term = over * zero[b], over * one[b] + pos * zero[b]
                                next_zero = zero_term if b == 0 else next_zero + zero_term
                                next_one = one_term if b == 0 else next_one + one_term
                            zero_to[pl.ds(out_base + a * out_stride + group, 8), at] = next_zero
                            one_to[pl.ds(out_base + a * out_stride + group, 8), at] = next_one

        stage_of(1, wide_in, wide_in * slot, slot, slot, wide_out * slot, zero_in, one_in, zero_out, one_out)
        stage_of(0, wide_out, slot, wide_out * slot, wide_out * slot, slot, zero_out, one_out, zero_in, one_in)
        live = wide_out**2 * slot
        out_size = wide_out**3
        over_tail, pos_tail = tails[(s, t)]
        totals[s][:, :out_size] += dot3(
            split(one_in[:live, :size]), split(over_tail[:, :out_size]), ((1,), (0,))
        ) + dot3(split(zero_in[:live, :size]), split(pos_tail[:, :out_size]), ((1,), (0,)))

    def first_sum(step):
        return pltpu.make_async_remote_copy(
            src_ref=sums,
            dst_ref=stage.at[place],
            send_sem=sum_send.at[step],
            recv_sem=sum_recv.at[step],
            device_id=device(layer, peer(step)),
            device_id_type=mesh_ids,
        )

    def second_sum(step):
        return pltpu.make_async_remote_copy(
            src_ref=layer_sums.at[layer],
            dst_ref=layer_sums.at[layer],
            send_sem=sum_send.at[wide + step],
            recv_sem=sum_recv.at[wide + step],
            device_id=device(lax.rem(layer + step, layers), place),
            device_id_type=mesh_ids,
        )

    barrier = pltpu.get_barrier_semaphore()
    for step in range(1, wide):
        pl.semaphore_signal(barrier, inc=1, device_id=device(layer, peer(step)), device_id_type=mesh_ids)
    for step in range(1, layers):
        pl.semaphore_signal(
            barrier, inc=1, device_id=device(lax.rem(layer + step, layers), place), device_id_type=mesh_ids
        )
    pl.semaphore_wait(barrier, wide + layers - 2)

    hops = layers - 1
    of = [[c for c in range(parts) if chunks[c][0] == t] for t in range(count)]
    line = of[3] + of[1] + of[2] + of[0]
    for c in line:
        keep(c).start()
        for step in range(1, wide):
            across(c, step).start()

    def begin(c):
        layer_ready(c)
        forward(c, 0)

    def relay(c, step):
        if step < hops:
            arrive(c, step - 1)
            forward(c, step)

    def local_begin(stage_at):
        if stage_at == 0:
            prepare()
            build_leads(3)
            build_leads(1)
        elif stage_at == 1:
            build_leads(2)
            build_leads(0)
        elif stage_at == 2:
            for s in range(count):
                cube(s)
                build_tail(s, s)
                for t in (s - 1, s + 1):
                    if 0 <= t < count:
                        build_tail(s, t)

    def close(s):
        flat(s)
        for c in of[s]:
            add_action(c)

    def local_after(c):
        if c in of[3]:
            self_part(0)
        elif c in of[1]:
            for s in range(1, count):
                self_part(s)
        elif c in of[2]:
            self_density(0)
        elif c == of[0][0]:
            for s in range(1, count):
                self_density(s)

    def collect(c):
        t = chunks[c][0]
        wait_home(c)
        if t:
            for s in (t - 1, t + 1):
                if 0 <= s < count:
                    pair_part(s, t)

    arrived = []
    for at in range(max(len(line) + hops, 3)):
        if at < len(line):
            begin(line[at])
        for step in range(1, hops):
            if 0 <= at - step < len(line):
                relay(line[at - step], step)
        local_begin(at)
        if at >= hops and at - hops < len(line):
            c = line[at - hops]
            if len(arrived) >= 3 and c != line[-1]:
                collect(arrived.pop(0))
            if hops:
                arrive(c, hops - 1)
            mix(c)
            local_after(c)
            if c == line[-1]:
                for step in range(1, wide):
                    first_sum(step).start()
                stage[place] = sums[...]
            send_home(c)
            arrived.append(c)
    done = []
    for c in arrived:
        if chunks[c][0] == 0 and not done:
            flat(0)
            close(2)
            close(3)
            for step in range(1, wide):
                first_sum(step).wait()
            layer_sums[layer] = jnp.sum(stage[...], axis=0)
            for step in range(1, layers):
                second_sum(step).start()
            done.append(c)
        collect(c)
        if chunks[c][0] == 0:
            add_action(c)
    pair_part(1, 0)
    close(1)
    for step in range(1, layers):
        second_sum(step).wait()
    sums_out[...] = jnp.sum(layer_sums[...], axis=0)

    for c in range(parts):
        for step in range(1, wide):
            across(c, step).wait_send()
            home(c, step).wait_send()
        for step in range(hops):
            for up in (True, False):
                @pl.when(sends_hop(step, up))
                def _():
                    hop(c, step, up).wait_send()


def call(kernel, outs, scratch, *args, name, remote=None):
    extra = params
    if remote is not None:
        extra = pltpu.CompilerParams(vmem_limit_bytes=vmem_limit, collective_id=remote, has_side_effects=True)
    return pl.pallas_call(
        kernel,
        out_shape=[jax.ShapeDtypeStruct(shape, jnp.float32) for shape in outs],
        in_specs=[vmem] * len(args),
        out_specs=[vmem] * len(outs),
        scratch_shapes=[pltpu.VMEM(shape, jnp.float32) if isinstance(shape, tuple) else shape for shape in scratch],
        compiler_params=extra,
        name=name,
    )(*args)


def round_up(value, unit):
    return -(-value // unit) * unit


def spread(table, rows, slot):
    shape = table.shape[:-1]
    held = table.reshape(shape + (-1, rows))
    wider = np.full(shape + (held.shape[-2], slot), -1 if table.dtype == np.int32 else 0, table.dtype)
    wider[..., :rows] = held
    return wider.reshape(shape + (-1,))


def local(*args):
    states = args[:4]
    operators = args[4:8]
    intersections, positions, coupling_pair, coupling_mode, coupling_strength = args[8:]
    devices = lax.axis_size("grp") * lax.axis_size("sub")
    count = len(states)
    widths = [operator.shape[1] for operator in operators]
    rows = [state.shape[0] for state in states]
    columns = [state.shape[1] for state in states]
    totals = [size * devices for size in rows]
    layers = max(1, lax.axis_size("grp") // 4)
    wide = devices // layers
    tiles = [-(-size // (wide * lanes)) for size in columns]
    slots = [round_up(size, 8) for size in rows]
    pairs, modes = intersections.shape[:2]

    combos = {}
    for p in range(pairs):
        combos[(p, p + 1)] = len(combos)
        combos[(p + 1, p)] = len(combos)
    for s in range(count):
        combos[(s, s)] = len(combos)

    order = [[(t, "pos")] + [(s, kind) for s in (t - 1, t + 1) if 0 <= s < count for kind in ("over", "pos")] for t in range(count)]
    kinds = list(dict.fromkeys(zip(widths, rows)))
    plan = [
        dict(
            rows=rows[t],
            slot=slots[t],
            tiles=tiles[t],
            columns=columns[t],
            width=widths[t],
            kind=kinds.index((widths[t], rows[t])),
            targets=[rows[s] for s, kind in order[t]],
        )
        for t in range(count)
    ]
    chunks = []
    for t in range(count):
        left, first = tiles[t], 0
        while left:
            number = -(-left // 2) if t == 0 and left == tiles[t] else left
            if t == 0 and left == tiles[t] and number > 8:
                number = 8
            if t == 0 and first and left > 4:
                number = -(-left // 2)
            chunks.append((t, first, number))
            first, left = first + number, left - number
    sends = call(
        functools.partial(pack_kernel, plan, chunks),
        [(wide, round_up(rows[t] * number, 8), lanes) for t, first, number in chunks],
        [],
        *states,
        name="pack",
    )
    back_shapes = [(wide, round_up(sum(plan[t]["targets"]) * number, 8), lanes) for t, first, number in chunks]
    coupling = jnp.stack(
        [coupling_pair.astype(jnp.float32), coupling_mode.astype(jnp.float32), coupling_strength]
    )
    tables = {name: [] for name in ("pick", "turned", "rest", "rest_turned")}
    for lead in (True, False):
        for width, held in kinds:
            size = held * devices if lead else width**3
            pick = np.zeros((3, 8, size), np.float32)
            rest = np.stack([others(width, 3, size, place) for place in range(3)])
            for place in range(3):
                pick[place, :width] = digits(width, 3, size, place)
            if lead:
                rest, pick = spread(rest, held, round_up(held, 8)), spread(pick, held, round_up(held, 8))
            tables["pick"].append(jnp.asarray(pick))
            tables["turned"].append(jnp.asarray(np.ascontiguousarray(pick.transpose(0, 2, 1))))
            tables["rest"].append(jnp.asarray(rest))
            tables["rest_turned"].append(jnp.asarray(np.ascontiguousarray(rest.T)))
    names = ("pick", "turned", "rest", "rest_turned")
    constants = [item for name in names for item in tables[name][: len(kinds)]] + [
        item for name in names for item in tables[name][len(kinds) :]
    ]
    cube_shapes = [(widths[s] ** 2 * slots[s], round_up(widths[s] ** 3, lanes)) for s in range(count)]
    mixed_shape = (max(widths) ** 2 * max(slots), round_up(max(widths) ** 3, lanes))
    depths = [devices * slots[t] for t in range(count)]
    dma = pltpu.SemaphoreType.DMA
    sum_shape = (8, count * 64)
    flowed = call(
        functools.partial(flow_kernel, plan, chunks, combos, layers, wide),
        [state.shape for state in states] + [sum_shape],
        [(layers,) + send.shape for send in sends]
        + back_shapes * 2
        + [(max(depths), max(number for t, first, number in chunks) * lanes), (wide * max(rows), 2 * lanes)]
        + [(wide * rows[s], depths[t]) for t in range(count) for s, kind in order[t]]
        + [(widths[t] ** 3, round_up(widths[s] ** 3, lanes)) for s, t in combos for _ in range(1 if s == t else 2)]
        + cube_shapes * 2
        + [mixed_shape] * 4
        + [(round_up(max(widths) ** 2, 8), max(depths + [mixed_shape[1]]))] * 2
        + [(max(totals), max(depths))] * 2
        + [(len(combos) * 16, 8, 8), (len(combos) * 256, lanes)]
        + [sum_shape, (wide,) + sum_shape, (layers,) + sum_shape, (8, mixed_shape[1])]
        + [dma((len(chunks), wide))] * 2
        + [dma((len(chunks), layers))] * 4
        + [dma((len(chunks), wide))] * 2
        + [dma((2 * len(chunks),))]
        + [dma((wide + layers,))] * 2,
        *sends,
        *states,
        jnp.transpose(intersections, (0, 2, 1, 3)),
        jnp.transpose(positions, (0, 2, 1, 3)),
        *[jnp.transpose(operator, (1, 0, 2)) for operator in operators],
        coupling,
        *constants,
        name="flow",
        remote=0,
    )
    finished = call(
        functools.partial(finish_kernel, count),
        [state.shape for state in states] + [(widths[t], modes, widths[t]) for t in range(count)],
        [],
        *states,
        *flowed,
        name="finish",
    )
    return tuple(finished[:count]) + tuple(jnp.transpose(item, (1, 0, 2)) for item in finished[count:])


def solution(mesh):
    sharded = P(("grp", "sub"), None)
    return jax.shard_map(
        local,
        mesh=mesh,
        in_specs=(sharded,) * 4 + (P(),) * 9,
        out_specs=(sharded,) * 4 + (P(),) * 4,
        check_vma=False,
    )
```

```python
import functools
import math

import jax
import jax.numpy as jnp
import numpy as np
from jax import lax
from jax.experimental import pallas as pl
from jax.experimental.pallas import tpu as pltpu
from jax.sharding import PartitionSpec as P

highest = lax.Precision.HIGHEST
time_step = 0.25
lanes = 128
vmem_limit = 63 * 1024 * 1024
params = pltpu.CompilerParams(vmem_limit_bytes=vmem_limit)
vmem = pl.BlockSpec(memory_space=pltpu.VMEM)
anywhere = pl.BlockSpec(memory_space=pl.ANY)
mesh_ids = pl.DeviceIdType.MESH


def digits(width, count, total, place):
    index = np.arange(total)
    live = index < width**count
    digit = (index // width ** (count - 1 - place)) % width
    return ((digit[None, :] == np.arange(width)[:, None]) & live[None, :]).astype(np.float32)


def others(width, count, total, place):
    index = np.arange(total)
    stride = width ** (count - 1 - place)
    rest = index - ((index // stride) % width) * stride
    return np.where(index < width**count, rest, -1).astype(np.int32)


def split(value):
    top = value.astype(jnp.bfloat16)
    return top, (value - top.astype(jnp.float32)).astype(jnp.bfloat16)


def dot3(left, right, contract):
    dims = (contract, ((), ()))
    go = functools.partial(lax.dot_general, dimension_numbers=dims, preferred_element_type=jnp.float32)
    return go(left[0], right[0]) + (go(left[0], right[1]) + go(left[1], right[0]))


def pack_kernel(plan, chunks, *refs):
    count = len(plan)
    sources = refs[:count]
    for out, (t, first, number) in zip(refs[count:], chunks):
        source, item = sources[t], plan[t]
        rows = item["rows"]
        used = number * rows
        if out.shape[1] > used:
            out[:, used:, :] = jnp.zeros((out.shape[0], out.shape[1] - used, lanes), jnp.float32)
        for device in range(out.shape[0]):
            for tile in range(number):
                start = (device * item["tiles"] + first + tile) * lanes
                width = min(lanes, item["columns"] - start)
                at = slice(tile * rows, (tile + 1) * rows)
                if width < lanes:
                    out[device, at, :] = jnp.zeros((rows, lanes), jnp.float32)
                if width > 0:
                    out[device, at, :width] = source[:, start : start + width]


def finish_kernel(count, *refs):
    states, changes, sums = refs[:count], refs[count : 2 * count], refs[2 * count]
    stepped, densities = refs[2 * count + 1 : 3 * count + 1], refs[3 * count + 1 :]
    for state, change, out in zip(states, changes, stepped):
        out[...] = state[...] - time_step * change[...]
    for t, out in enumerate(densities):
        width, modes = out.shape[:2]
        for mode in range(modes):
            at = (t * 8 + mode) * 8
            out[:, mode, :] = sums[:width, at : at + width] * (1.0 / float(width ** (modes - 1)))


def flow_kernel(plan, chunks, combos, layers, wide, *refs):
    count = len(plan)
    spare = list(refs)

    def take(number):
        taken = spare[:number]
        del spare[:number]
        return taken

    parts = len(chunks)
    sends, states_far = take(parts), take(count)
    intersections, positions = take(2)
    operators = take(count)
    coupling_pair, coupling_mode, coupling_strength = take(3)
    kinds = [item["kind"] for item in plan]
    tables_far = [take(max(kinds) + 1) for _ in range(8)]
    changes = take(count)
    (sums_out,) = take(1)
    gathered, mixed, back = take(parts), take(parts), take(parts)
    value, result = take(2)
    matrices = [take(len(item["targets"])) for item in plan]
    tails = {key: take(1 if key[0] == key[1] else 2) for key in combos}
    cubes, totals = take(count), take(count)
    zero_in, one_in, zero_out, one_out = take(4)
    inner_over, inner_pos, full_over, full_pos = take(4)
    small, splats, sums, stage, layer_sums, rows_of_sums = take(6)
    states = take(count)
    tables_near = {which: take(max(kinds) + 1) for which in (1, 3, 5, 7)}
    tables = [tables_near.get(which, table) for which, table in enumerate(tables_far)]
    lead_pick, lead_turned, lead_rest, lead_rest_turned, tail_pick, tail_turned, tail_rest, tail_rest_turned = [
        [table[kind] for kind in kinds] for table in tables
    ]
    loads = list(zip(states_far, states))
    for which in tables_near:
        loads += list(zip(tables_far[which], tables_near[which]))
    across_send, across_recv, up_send, up_recv, down_send, down_recv, home_send, home_recv, own, sum_send, sum_recv, load = spare
    fetches = [pltpu.make_async_copy(far, near, load.at[at]) for at, (far, near) in enumerate(loads)]

    sub = lax.axis_size("sub")
    me = lax.axis_index("grp") * sub + lax.axis_index("sub")
    layer, place = me // wide, me % wide

    def device(at_layer, at_place):
        index = at_layer * wide + at_place
        return (index // sub, index % sub)

    def peer(step):
        return lax.rem(place + step, wide)

    def across(t, step):
        return pltpu.make_async_remote_copy(
            src_ref=sends[t].at[peer(step)],
            dst_ref=gathered[t].at[layer, place],
            send_sem=across_send.at[t, step],
            recv_sem=across_recv.at[t, step],
            device_id=device(layer, peer(step)),
            device_id_type=mesh_ids,
        )

    def home(t, step):
        return pltpu.make_async_remote_copy(
            src_ref=mixed[t].at[peer(step)],
            dst_ref=back[t].at[place],
            send_sem=home_send.at[t, step],
            recv_sem=home_recv.at[t, step],
            device_id=device(layer, peer(step)),
            device_id_type=mesh_ids,
        )

    def hop(t, step, up):
        block = layer - step if up else layer + step
        return pltpu.make_async_remote_copy(
            src_ref=gathered[t].at[block],
            dst_ref=gathered[t].at[block],
            send_sem=(up_send if up else down_send).at[t, step],
            recv_sem=(up_recv if up else down_recv).at[t, step],
            device_id=device(layer + 1 if up else layer - 1, place),
            device_id_type=mesh_ids,
        )

    def sends_hop(step, up):
        if up:
            return jnp.logical_and(layer - step >= 0, layer + 1 < layers)
        return jnp.logical_and(layer + step < layers, layer >= 1)

    def forward(t, step):
        for up in (True, False):
            @pl.when(sends_hop(step, up))
            def _():
                hop(t, step, up).start()

    def arrive(t, step):
        @pl.when(layer - 1 - step >= 0)
        def _():
            pltpu.make_async_remote_copy(
                src_ref=gathered[t].at[layer - 1 - step],
                dst_ref=gathered[t].at[layer - 1 - step],
                send_sem=up_send.at[t, step],
                recv_sem=up_recv.at[t, step],
                device_id=device(layer - 1, place),
                device_id_type=mesh_ids,
            ).wait_recv()

        @pl.when(layer + 1 + step < layers)
        def _():
            pltpu.make_async_remote_copy(
                src_ref=gathered[t].at[layer + 1 + step],
                dst_ref=gathered[t].at[layer + 1 + step],
                send_sem=down_send.at[t, step],
                recv_sem=down_recv.at[t, step],
                device_id=device(layer + 1, place),
                device_id_type=mesh_ids,
            ).wait_recv()

    def keep(t):
        return pltpu.make_async_copy(sends[t].at[place], gathered[t].at[layer, place], own.at[t])

    def keep_home(t):
        return pltpu.make_async_copy(mixed[t].at[place], back[t].at[place], own.at[parts + t])

    def layer_ready(t):
        keep(t).wait()
        for step in range(1, wide):
            across(t, step).wait_recv()

    def put_density(more, t, mode, block):
        at = (t * 8 + mode) * 8
        sums[:, at : at + 8] = sums[:, at : at + 8] + block if more else block

    def add_density(more, t, mode, gram, rest_rows, rest_columns, pick, turned):
        kept = split(jnp.where(rest_rows == rest_columns, gram, 0.0))
        chosen = pick.astype(jnp.bfloat16)
        dims = (((1,), (1,)), ((), ()))
        right = lax.dot_general(kept[0], chosen, dims, preferred_element_type=jnp.float32) + lax.dot_general(
            kept[1], chosen, dims, preferred_element_type=jnp.float32
        )
        block = lax.dot_general(
            turned, right, (((0,), (0,)), ((), ())), precision=highest, preferred_element_type=jnp.float32
        )
        put_density(more, t, mode, 0.5 * (block + block.T))

    def mix(c):
        t, first, tiles = chunks[c]
        item = plan[t]
        rows, slot = item["rows"], item["slot"]
        depth = layers * wide * slot
        value[:depth, : tiles * lanes] = jnp.zeros((depth, tiles * lanes), jnp.float32)

        @pl.loop(0, layers)
        def _(at_layer):
            @pl.loop(0, wide)
            def _(at_place):
                base = pl.multiple_of((at_layer * wide + at_place) * slot, slot)
                for tile in range(tiles):
                    value[pl.ds(base, rows), tile * lanes : (tile + 1) * lanes] = gathered[c][
                        at_layer, at_place, tile * rows : (tile + 1) * rows, :
                    ]

        blocks = []
        for matrix in matrices[t]:
            blocks.append(split(matrix[...]))
        mine = pl.ds(pl.multiple_of(layer * wide * slot, 8), wide * slot)
        gram = None
        for start in range(0, tiles, 2):
            wide_tiles = min(2, tiles - start)
            span = slice(start * lanes, (start + wide_tiles) * lanes)
            data = split(value[:depth, span])
            own_rows = split(value[mine, span])
            part = lax.dot_general(
                own_rows[0], data[0], (((1,), (1,)), ((), ())), preferred_element_type=jnp.float32
            ) + 2.0 * lax.dot_general(
                own_rows[0], data[1], (((1,), (1,)), ((), ())), preferred_element_type=jnp.float32
            )
            gram = part if gram is None else gram + part
            offset = 0
            for block, target in zip(blocks, item["targets"]):
                size = target * wide
                result[:size, : wide_tiles * lanes] = dot3(block, data, ((1,), (0,)))
                for at_place in range(wide):
                    for tile in range(wide_tiles):
                        row = offset + (start + tile) * target
                        mixed[c][at_place, row : row + target, :] = result[
                            at_place * target : (at_place + 1) * target, tile * lanes : (tile + 1) * lanes
                        ]
                offset += target * tiles
        if mixed[c].shape[1] > offset:
            mixed[c][:, offset:, :] = jnp.zeros((wide, mixed[c].shape[1] - offset, lanes), jnp.float32)
        for k in range(3):
            turned = lead_turned[t][k, mine, :]
            add_density(first > 0, t, k, gram, lead_rest_turned[t][mine, k : k + 1], lead_rest[t][k : k + 1, :], lead_pick[t][k], turned)

    def send_home(t):
        keep_home(t).start()
        for step in range(1, wide):
            home(t, step).start()

    def expand(key, kind, mode, pick):
        matrix = small[(combos[key] * 2 + kind) * 8 + mode]
        out = None
        for b in range(plan[key[1]]["width"]):
            term = matrix[:, b : b + 1] * pick[b : b + 1, :]
            out = term if out is None else out + term
        return out

    def build(key, picks, mode, over_out, pos_out, rows):
        width = plan[key[0]]["width"]
        cols = picks.shape[-1]
        over = [expand(key, 0, mode + k, picks[k]) for k in range(3)]
        pos = [expand(key, 1, mode + k, picks[k]) for k in range(3)]
        square = width * width
        if rows > square * width:
            for out in (over_out, pos_out):
                if out is not None:
                    out[square * width : rows, :cols] = jnp.zeros((rows - square * width, cols), jnp.float32)
        for a in range(width):
            span = slice(a * width, (a + 1) * width)
            inner_over[span, :cols] = over[1][a : a + 1] * over[2][:width]
            inner_pos[span, :cols] = pos[1][a : a + 1] * over[2][:width] + over[1][a : a + 1] * pos[2][:width]
        over_value = inner_over[:square, :cols]
        pos_value = inner_pos[:square, :cols]
        for a in range(width):
            span = slice(a * square, (a + 1) * square)
            pos_out[span, :cols] = pos[0][a : a + 1] * over_value + over[0][a : a + 1] * pos_value
            if over_out is not None:
                over_out[span, :cols] = over[0][a : a + 1] * over_value

    def build_leads(t):
        cols = plan[t]["slot"] * layers * wide
        sources = [t] + [s for s in (t - 1, t + 1) if 0 <= s < count]
        at = 0
        for s in sources:
            rows = plan[s]["rows"]
            build((s, t), lead_pick[t], 0, full_over if s != t else None, full_pos, rows * layers * wide)
            mine = pl.ds(pl.multiple_of(layer * rows * wide, 8), rows * wide)
            for full in (full_over, full_pos) if s != t else (full_pos,):
                matrices[t][at][...] = full[mine, :cols]
                at += 1

    def build_tail(s, t):
        outs = tails[(s, t)]
        build((t, s), tail_pick[s], 5, outs[0] if s != t else None, outs[-1], plan[t]["width"] ** 3)

    def cube(s):
        item = plan[s]
        rows, slot, width = item["rows"], item["slot"], item["width"]
        size = width**3
        cubes[s][...] = jnp.zeros(cubes[s].shape, jnp.float32)
        for q in range(width**2):
            cubes[s][q * slot : q * slot + rows, :size] = states[s][:, q * size : (q + 1) * size]

    def scalar(key, kind, mode, a, b):
        row = ((combos[key] * 2 + kind) * 2 + mode) * 64 + b * 8 + a
        return splats[row : row + 1, :]

    def prepare():
        small[...] = jnp.zeros(small.shape, jnp.float32)
        pair, mode_of, strength = coupling_pair[...], coupling_mode[...], coupling_strength[...]
        for p in range(count - 1):
            rows, cols = plan[p]["width"], plan[p + 1]["width"]
            for k in range(8):
                chosen = jnp.logical_and(pair == p, mode_of == k)
                weight = jnp.sum(jnp.where(chosen, strength, 0.0), axis=1, keepdims=True)
                for kind, source in enumerate((intersections, positions)):
                    block = source[p, :rows, k, :cols]
                    if kind:
                        block = weight * block
                    at = (combos[(p, p + 1)] * 2 + kind) * 8 + k
                    small[at, :rows, :cols] = block
                    small[(combos[(p + 1, p)] * 2 + kind) * 8 + k] = small[at].T
        row = lax.broadcasted_iota(jnp.int32, (8, 8), 0)
        column = lax.broadcasted_iota(jnp.int32, (8, 8), 1)
        for t in range(count):
            width = plan[t]["width"]
            unit = jnp.where(jnp.logical_and(row == column, row < width), 1.0, 0.0)
            for k in range(8):
                small[combos[(t, t)] * 16 + k] = unit
                at = combos[(t, t)] * 16 + 8 + k
                small[at, :width, :width] = operators[t][:, k, :]
                if k >= 5:
                    small[at] = small[at].T
        for key in combos:
            for kind in range(2):
                for mode in range(2):
                    matrix = small[(combos[key] * 2 + kind) * 8 + 3 + mode]
                    base = ((combos[key] * 2 + kind) * 2 + mode) * 64
                    for b in range(8):
                        splats[base + b * 8 : base + b * 8 + 8, :] = jnp.broadcast_to(matrix[:, b : b + 1], (8, lanes))

    def self_part(s):
        item = plan[s]
        slot, width = item["slot"], item["width"]
        size = width**3
        total = totals[s]
        total[:, :size] = dot3(split(cubes[s][:, :size]), split(tails[(s, s)][0][:, :size]), ((1,), (0,)))
        block = width * slot
        for tile in range(-(-size // lanes)):
            at = slice(tile * lanes, (tile + 1) * lanes)

            @pl.loop(0, width)
            def _(i):
                base = pl.multiple_of(i * block, 8)
                held = [cubes[s][pl.ds(base + b * slot, slot), at] for b in range(width)]
                for a in range(width):
                    out = total[pl.ds(base + a * slot, slot), at]
                    for b in range(width):
                        out = out + scalar((s, s), 1, 1, a, b) * held[b]
                    total[pl.ds(base + a * slot, slot), at] = out

            @pl.loop(0, width)
            def _(i):
                base = pl.multiple_of(i * slot, 8)
                held = [cubes[s][pl.ds(base + b * block, slot), at] for b in range(width)]
                for a in range(width):
                    out = total[pl.ds(base + a * block, slot), at]
                    for b in range(width):
                        out = out + scalar((s, s), 1, 0, a, b) * held[b]
                    total[pl.ds(base + a * block, slot), at] = out

    def self_density(s):
        item = plan[s]
        slot, width = item["slot"], item["width"]
        size = width**3
        data = split(cubes[s][:, :size])
        gram = None
        step = width * slot
        dims = (((0,), (0,)), ((), ()))
        gram = lax.dot_general(data[0], data[0], dims, preferred_element_type=jnp.float32) + 2.0 * lax.dot_general(
            data[0], data[1], dims, preferred_element_type=jnp.float32
        )
        for k in range(3):
            add_density(
                False, s, 5 + k, gram, tail_rest_turned[s][:, k : k + 1], tail_rest[s][k : k + 1, :], tail_pick[s][k], tail_turned[s][k]
            )
        column = lax.broadcasted_iota(jnp.int32, (8, 8), 1)
        wide_lanes = cubes[s].shape[1]
        rows_of_sums[...] = jnp.zeros(rows_of_sums.shape, jnp.float32)
        for mode in range(2):
            block = jnp.zeros((8, 8), jnp.float32)
            for i in range(width):
                for j in range(width):
                    row = None
                    for other in range(width):
                        left = (i * width + other if mode == 0 else other * width + i) * slot
                        right = (j * width + other if mode == 0 else other * width + j) * slot
                        term = cubes[s][left : left + slot, :] * cubes[s][right : right + slot, :]
                        row = term if row is None else row + term
                    rows_of_sums[j : j + 1, :wide_lanes] = jnp.sum(row, axis=0, keepdims=True)
                column_sum = jnp.sum(rows_of_sums[:, :wide_lanes], axis=1, keepdims=True)
                block = jnp.where(column == i, column_sum, block)
            put_density(False, s, 3 + mode, block)

    def pieces(c):
        t, first, tiles = chunks[c]
        columns, size = plan[t]["columns"], plan[t]["width"] ** 3
        out = []
        for at_place in range(wide):
            for tile in range(tiles):
                start = (at_place * plan[t]["tiles"] + first + tile) * lanes
                stop = min(start + lanes, columns)
                while start < stop:
                    q = start // size
                    end = min(stop, (q + 1) * size)
                    out.append((at_place, tile, start % lanes, end - start, q, start - q * size))
                    start = end
        return out

    def wait_home(c):
        keep_home(c).wait()
        for step in range(1, wide):
            home(c, step).wait_recv()

    def flat(s):
        item = plan[s]
        rows, slot, size = item["rows"], item["slot"], item["width"] ** 3
        for q in range(item["width"] ** 2):
            changes[s][:, q * size : (q + 1) * size] = totals[s][q * slot : q * slot + rows, :size]

    def add_action(c):
        t, first, tiles = chunks[c]
        item = plan[t]
        rows = item["rows"]
        for at_place in range(wide):
            for tile in range(tiles):
                start = (at_place * item["tiles"] + first + tile) * lanes
                width = min(lanes, item["columns"] - start)
                if width > 0:
                    changes[t][:, start : start + width] += back[c][at_place, tile * rows : (tile + 1) * rows, :width]

    def pair_part(s, t):
        item = plan[t]
        rows, slot = plan[s]["rows"], plan[s]["slot"]
        wide_in, wide_out, size = item["width"], plan[s]["width"], item["width"] ** 3
        before = item["rows"]
        if s > t and t > 0:
            before += 2 * plan[t - 1]["rows"]
        for c, chunk in enumerate(chunks):
            if chunk[0] != t:
                continue
            offset = before * chunk[2]
            for target in (zero_in, one_in):
                for at_place, tile, lane, length, q, inside in pieces(c):
                    row = offset + tile * rows
                    target[q * slot : q * slot + rows, inside : inside + length] = back[c][
                        at_place, row : row + rows, lane : lane + length
                    ]
                offset += rows * chunk[2]

        def stage_of(mode, loops, step, in_stride, out_stride, out_step, zero_from, one_from, zero_to, one_to):
            for tile in range(-(-size // lanes)):
                at = slice(tile * lanes, (tile + 1) * lanes)

                @pl.loop(0, loops)
                def _(i):
                    base = pl.multiple_of(i * step, 8)
                    out_base = pl.multiple_of(i * out_step, 8)
                    for group in range(0, slot, 8):
                        zero = [zero_from[pl.ds(base + b * in_stride + group, 8), at] for b in range(wide_in)]
                        one = [one_from[pl.ds(base + b * in_stride + group, 8), at] for b in range(wide_in)]
                        for a in range(wide_out):
                            next_zero, next_one = None, None
                            for b in range(wide_in):
                                over, pos = scalar((s, t), 0, mode, a, b), scalar((s, t), 1, mode, a, b)
                                zero_term, one_term = over * zero[b], over * one[b] + pos * zero[b]
                                next_zero = zero_term if b == 0 else next_zero + zero_term
                                next_one = one_term if b == 0 else next_one + one_term
                            zero_to[pl.ds(out_base + a * out_stride + group, 8), at] = next_zero
                            one_to[pl.ds(out_base + a * out_stride + group, 8), at] = next_one

        stage_of(1, wide_in, wide_in * slot, slot, slot, wide_out * slot, zero_in, one_in, zero_out, one_out)
        stage_of(0, wide_out, slot, wide_out * slot, wide_out * slot, slot, zero_out, one_out, zero_in, one_in)
        live = wide_out**2 * slot
        out_size = wide_out**3
        over_tail, pos_tail = tails[(s, t)]
        totals[s][:, :out_size] += dot3(
            split(one_in[:live, :size]), split(over_tail[:, :out_size]), ((1,), (0,))
        ) + dot3(split(zero_in[:live, :size]), split(pos_tail[:, :out_size]), ((1,), (0,)))

    def first_sum(step):
        return pltpu.make_async_remote_copy(
            src_ref=sums,
            dst_ref=stage.at[place],
            send_sem=sum_send.at[step],
            recv_sem=sum_recv.at[step],
            device_id=device(layer, peer(step)),
            device_id_type=mesh_ids,
        )

    def second_sum(step):
        return pltpu.make_async_remote_copy(
            src_ref=layer_sums.at[layer],
            dst_ref=layer_sums.at[layer],
            send_sem=sum_send.at[wide + step],
            recv_sem=sum_recv.at[wide + step],
            device_id=device(lax.rem(layer + step, layers), place),
            device_id_type=mesh_ids,
        )

    for fetch in fetches:
        fetch.start()
    barrier = pltpu.get_barrier_semaphore()
    for step in range(1, wide):
        pl.semaphore_signal(barrier, inc=1, device_id=device(layer, peer(step)), device_id_type=mesh_ids)
    for step in range(1, layers):
        pl.semaphore_signal(
            barrier, inc=1, device_id=device(lax.rem(layer + step, layers), place), device_id_type=mesh_ids
        )
    pl.semaphore_wait(barrier, wide + layers - 2)

    hops = layers - 1
    of = [[c for c in range(parts) if chunks[c][0] == t] for t in range(count)]
    line = of[3] + of[1] + of[2] + of[0]
    for c in line:
        keep(c).start()
        for step in range(1, wide):
            across(c, step).start()

    def begin(c):
        layer_ready(c)
        forward(c, 0)

    def relay(c, step):
        if step < hops:
            arrive(c, step - 1)
            forward(c, step)

    def local_begin(stage_at):
        if stage_at == 0:
            prepare()
            build_leads(3)
            build_leads(1)
        elif stage_at == 1:
            build_leads(2)
            build_leads(0)
        elif stage_at == 2:
            for fetch in fetches:
                fetch.wait()
            for s in range(count):
                cube(s)
                build_tail(s, s)
                for t in (s - 1, s + 1):
                    if 0 <= t < count:
                        build_tail(s, t)

    def close(s):
        flat(s)
        for c in of[s]:
            add_action(c)

    def local_after(c):
        if c in of[3]:
            self_part(0)
        elif c in of[1]:
            for s in range(1, count):
                self_part(s)
        elif c in of[2]:
            self_density(0)
        elif c == of[0][0]:
            for s in range(1, count):
                self_density(s)

    def collect(c):
        t = chunks[c][0]
        wait_home(c)
        if t:
            for s in (t - 1, t + 1):
                if 0 <= s < count:
                    pair_part(s, t)

    arrived, closed = [], []
    for at in range(max(len(line) + hops, 3)):
        if at < len(line):
            begin(line[at])
        for step in range(1, hops):
            if 0 <= at - step < len(line):
                relay(line[at - step], step)
        local_begin(at)
        if at >= hops and at - hops < len(line):
            c = line[at - hops]
            if len(arrived) >= 3:
                collect(arrived.pop(0))
            if c == line[-1] and not any(chunks[other][0] for other in arrived):
                flat(0)
                close(2)
                close(3)
                closed.append(c)
            if hops:
                arrive(c, hops - 1)
            mix(c)
            local_after(c)
            if c == line[-1]:
                for step in range(1, wide):
                    first_sum(step).start()
                stage[place] = sums[...]
            send_home(c)
            arrived.append(c)
    done = []
    for c in arrived:
        if chunks[c][0] == 0 and not done:
            if not closed:
                flat(0)
                close(2)
                close(3)
            for step in range(1, wide):
                first_sum(step).wait()
            layer_sums[layer] = jnp.sum(stage[...], axis=0)
            for step in range(1, layers):
                second_sum(step).start()
            done.append(c)
        collect(c)
        if chunks[c][0] == 0:
            add_action(c)
    pair_part(1, 0)
    close(1)
    for step in range(1, layers):
        second_sum(step).wait()
    sums_out[...] = jnp.sum(layer_sums[...], axis=0)

    for c in range(parts):
        for step in range(1, wide):
            across(c, step).wait_send()
            home(c, step).wait_send()
        for step in range(hops):
            for up in (True, False):
                @pl.when(sends_hop(step, up))
                def _():
                    hop(c, step, up).wait_send()


def call(kernel, outs, scratch, *args, name, remote=None, far=()):
    extra = params
    if remote is not None:
        extra = pltpu.CompilerParams(vmem_limit_bytes=vmem_limit, collective_id=remote, has_side_effects=True)
    return pl.pallas_call(
        kernel,
        out_shape=[jax.ShapeDtypeStruct(shape, jnp.float32) for shape in outs],
        in_specs=[anywhere if at in far else vmem for at in range(len(args))],
        out_specs=[vmem] * len(outs),
        scratch_shapes=[
            pltpu.VMEM(shape, jnp.float32)
            if isinstance(shape, tuple)
            else pltpu.VMEM(shape.shape, shape.dtype)
            if isinstance(shape, jax.ShapeDtypeStruct)
            else shape
            for shape in scratch
        ],
        compiler_params=extra,
        name=name,
    )(*args)


def round_up(value, unit):
    return -(-value // unit) * unit


def spread(table, rows, slot):
    shape = table.shape[:-1]
    held = table.reshape(shape + (-1, rows))
    wider = np.full(shape + (held.shape[-2], slot), -1 if table.dtype == np.int32 else 0, table.dtype)
    wider[..., :rows] = held
    return wider.reshape(shape + (-1,))


def local(*args):
    states = args[:4]
    operators = args[4:8]
    intersections, positions, coupling_pair, coupling_mode, coupling_strength = args[8:]
    devices = lax.axis_size("grp") * lax.axis_size("sub")
    count = len(states)
    widths = [operator.shape[1] for operator in operators]
    rows = [state.shape[0] for state in states]
    columns = [state.shape[1] for state in states]
    totals = [size * devices for size in rows]
    layers = max(1, lax.axis_size("grp") // 4)
    wide = devices // layers
    tiles = [-(-size // (wide * lanes)) for size in columns]
    slots = [round_up(size, 8) for size in rows]
    pairs, modes = intersections.shape[:2]

    combos = {}
    for p in range(pairs):
        combos[(p, p + 1)] = len(combos)
        combos[(p + 1, p)] = len(combos)
    for s in range(count):
        combos[(s, s)] = len(combos)

    order = [[(t, "pos")] + [(s, kind) for s in (t - 1, t + 1) if 0 <= s < count for kind in ("over", "pos")] for t in range(count)]
    kinds = list(dict.fromkeys(zip(widths, rows)))
    plan = [
        dict(
            rows=rows[t],
            slot=slots[t],
            tiles=tiles[t],
            columns=columns[t],
            width=widths[t],
            kind=kinds.index((widths[t], rows[t])),
            targets=[rows[s] for s, kind in order[t]],
        )
        for t in range(count)
    ]
    chunks = []
    for t in range(count):
        left, first = tiles[t], 0
        while left:
            number = -(-left // 2) if t == 0 and left == tiles[t] else left
            if t == 0 and left == tiles[t] and number > 8:
                number = 8
            if t == 0 and first and left > 4:
                number = -(-left // 2)
            chunks.append((t, first, number))
            first, left = first + number, left - number
    sends = call(
        functools.partial(pack_kernel, plan, chunks),
        [(wide, round_up(rows[t] * number, 8), lanes) for t, first, number in chunks],
        [],
        *states,
        name="pack",
    )
    back_shapes = [(wide, round_up(sum(plan[t]["targets"]) * number, 8), lanes) for t, first, number in chunks]
    tables = {name: [] for name in ("pick", "turned", "rest", "rest_turned")}
    for lead in (True, False):
        for width, held in kinds:
            size = held * devices if lead else width**3
            pick = np.zeros((3, 8, size), np.float32)
            rest = np.stack([others(width, 3, size, place) for place in range(3)])
            for place in range(3):
                pick[place, :width] = digits(width, 3, size, place)
            if lead:
                rest, pick = spread(rest, held, round_up(held, 8)), spread(pick, held, round_up(held, 8))
            tables["pick"].append(jnp.asarray(pick))
            tables["turned"].append(jnp.asarray(np.ascontiguousarray(pick.transpose(0, 2, 1))))
            tables["rest"].append(jnp.asarray(rest))
            tables["rest_turned"].append(jnp.asarray(np.ascontiguousarray(rest.T)))
    names = ("pick", "turned", "rest", "rest_turned")
    constants = [item for name in names for item in tables[name][: len(kinds)]] + [
        item for name in names for item in tables[name][len(kinds) :]
    ]
    cube_shapes = [(widths[s] ** 2 * slots[s], round_up(widths[s] ** 3, lanes)) for s in range(count)]
    mixed_shape = (max(widths) ** 2 * max(slots), round_up(max(widths) ** 3, lanes))
    depths = [devices * slots[t] for t in range(count)]
    dma = pltpu.SemaphoreType.DMA
    sum_shape = (8, count * 64)
    states_at = len(chunks)
    tables_at = states_at + 2 * count + 5
    far = set(range(states_at, states_at + count))
    far |= {tables_at + at * len(kinds) + kind for at in (1, 3, 5, 7) for kind in range(len(kinds))}
    flowed = call(
        functools.partial(flow_kernel, plan, chunks, combos, layers, wide),
        [state.shape for state in states] + [sum_shape],
        [(layers,) + send.shape for send in sends]
        + back_shapes * 2
        + [(max(depths), max(number for t, first, number in chunks) * lanes), (wide * max(rows), 2 * lanes)]
        + [(wide * rows[s], depths[t]) for t in range(count) for s, kind in order[t]]
        + [(widths[t] ** 3, round_up(widths[s] ** 3, lanes)) for s, t in combos for _ in range(1 if s == t else 2)]
        + cube_shapes * 2
        + [mixed_shape] * 4
        + [(round_up(max(widths) ** 2, 8), max(depths + [mixed_shape[1]]))] * 2
        + [(max(totals), max(depths))] * 2
        + [(len(combos) * 16, 8, 8), (len(combos) * 256, lanes)]
        + [sum_shape, (wide,) + sum_shape, (layers,) + sum_shape, (8, mixed_shape[1])]
        + [state.shape for state in states]
        + [
            jax.ShapeDtypeStruct(constants[at * len(kinds) + kind].shape, constants[at * len(kinds) + kind].dtype)
            for at in (1, 3, 5, 7)
            for kind in range(len(kinds))
        ]
        + [dma((len(chunks), wide))] * 2
        + [dma((len(chunks), layers))] * 4
        + [dma((len(chunks), wide))] * 2
        + [dma((2 * len(chunks),))]
        + [dma((wide + layers,))] * 2
        + [dma((count + 4 * len(kinds),))],
        *sends,
        *states,
        jnp.transpose(intersections, (0, 2, 1, 3)),
        jnp.transpose(positions, (0, 2, 1, 3)),
        *[jnp.transpose(operator, (1, 0, 2)) for operator in operators],
        coupling_pair[None, :],
        coupling_mode[None, :],
        coupling_strength[None, :],
        *constants,
        name="flow",
        remote=0,
        far=far,
    )
    finished = call(
        functools.partial(finish_kernel, count),
        [state.shape for state in states] + [(widths[t], modes, widths[t]) for t in range(count)],
        [],
        *states,
        *flowed,
        name="finish",
    )
    return tuple(finished[:count]) + tuple(jnp.transpose(item, (1, 0, 2)) for item in finished[count:])


def solution(mesh):
    sharded = P(("grp", "sub"), None)
    return jax.shard_map(
        local,
        mesh=mesh,
        in_specs=(sharded,) * 4 + (P(),) * 9,
        out_specs=(sharded,) * 4 + (P(),) * 4,
        check_vma=False,
    )
```
